32 devices in a mesh: groups: 2 (over y), tensor: 4 (over z), dp: 4 (over x, core).
Axes of the slice: x: 2, y: 2, z: 4, core: 2. Of those that a mesh axis runs over, the one named last changes fastest.
Arguments:
- out_grad: bfloat16 [4, 1280, 4096], P('dp', ('groups', 'tensor')), parts along dimension 1, may hold values from -6 to 6
- gate_pre: bfloat16 [4, 1280, 14336], P('dp', 'groups', 'tensor'), parts along dimension 1, may hold values from -8 to 8
- up_pre: bfloat16 [4, 1280, 14336], P('dp', 'groups', 'tensor'), parts along dimension 1, may hold values from -6 to 6
- down_weight: bfloat16 [14336, 4096], P('tensor'), may hold values from -0.046875 to 0.046875
Outputs:
- gate_grad: bfloat16 [4, 1280, 14336], P('dp', 'groups', 'tensor'), parts along dimension 1
- up_grad: bfloat16 [4, 1280, 14336], P('dp', 'groups', 'tensor'), parts along dimension 1
- down_grad: bfloat16 [28672, 4096], P(('groups', 'tensor'), 'dp'), parts along dimension 0
The draws below stay inside these ranges and needn't reach their ends.
There are 2 independent parts, one for each index of `groups`. The reference program is written for one: setup_inputs(seed, part) draws one part's arguments, and reference() takes and returns one part's arrays. A program takes and returns all parts, laid end to end along the dimension named above; an argument that names none is the same for every part. Nothing has to cross between parts.
All inputs are finite; a program needn't handle non-finite values.
Results may differ from the reference program's by a relative error of at most 0.014.
Values may be sent and summed in bfloat16 or wider, within the bound.
A program may use at most 128 MiB of HBM per device.

```python
import math
import jax
import jax.numpy as jnp
from jax import lax

D = 4096
FF = 14336
TOK_GROUP = 640
DATA = 4
TOKENS = 2560


def block_scale(rng, extent, pieces, low, high):
    gain, own = 1.0, jax.random.fold_in(rng, 6)
    for position, parts in pieces:
        draws = jnp.exp(jax.random.uniform(jax.random.fold_in(own, position), (parts,), jnp.float32, low / len(pieces), high / len(pieces)))
        gain = gain * jnp.repeat(draws, extent[position] // parts).reshape([-1 if axis == position else 1 for axis in range(len(extent))])
    return gain


def centred(rng, extent, width, reach, pieces=(), kind=jnp.bfloat16):
    level = block_scale(rng, extent, pieces, -0.22, 0.18) if pieces else 1.0
    drawn = jax.random.normal(rng, extent, jnp.float32) * width * level
    return jnp.minimum(jnp.maximum(drawn, -reach), reach).astype(kind)


def setup_inputs(seed: int = 0, part: int = 0) -> dict:
    arg_keys = jax.random.split(jax.random.key(seed), 5)
    own_keys = jax.random.split(jax.random.fold_in(arg_keys[4], part), 5)
    return {
        "out_grad": centred(own_keys[0], (DATA, TOK_GROUP, D), 1.0, 6.0, ((0, 4), (1, 4))),
        "gate_pre": centred(own_keys[1], (DATA, TOK_GROUP, FF), 1.5, 8.0, ((0, 4), (2, 4))),
        "up_pre": centred(own_keys[2], (DATA, TOK_GROUP, FF), 1.0, 6.0, ((0, 4), (2, 4))),
        "down_weight": centred(arg_keys[3], (FF, D), FF ** -0.5, 0.046875, ((0, 4),)),
    }


def reference(out_grad, gate_pre, up_pre, down_weight):
    gate = gate_pre.astype(jnp.float32)
    up = up_pre.astype(jnp.float32)
    sig = jax.nn.sigmoid(gate)
    act = gate * sig
    hidden = (act * up).astype(jnp.bfloat16)
    scale = 1.0 / math.sqrt(TOKENS)
    indices = jnp.arange(DATA)

    def group_term(total, index):
        term = jnp.dot(hidden[index].T, out_grad[index], preferred_element_type=jnp.float32) * scale
        rounded = lax.optimization_barrier(term.astype(jnp.bfloat16))
        return (total + rounded.astype(jnp.float32), None)
    total, _ = lax.scan(group_term, jnp.zeros((FF, D), jnp.float32), indices)

    def group_grad(index):
        return jnp.dot(out_grad[index], down_weight.T, preferred_element_type=jnp.float32)
    hidden_grad = lax.map(group_grad, indices)
    gate_grad = (hidden_grad * up * sig * (1.0 + gate * (1.0 - sig))).astype(jnp.bfloat16)
    up_grad = (hidden_grad * act).astype(jnp.bfloat16)
    return (gate_grad, up_grad, total.astype(jnp.bfloat16))
```

```python
import functools
import math

import jax
import jax.numpy as jnp
from jax import lax
from jax.experimental import pallas as pl
from jax.experimental.pallas import tpu as pltpu
from jax.sharding import PartitionSpec as P

A_PIECES = 4
PARTS = 2
MESH = pl.DeviceIdType.MESH


def exchange(
    nt, nx, tile, scale,
    og, gate, up, weight,
    gate_grad, up_grad, down_grad,
    og_v, xb_v, hid_v, cols_v, acc_v,
    own_sem, a_recv, a_up, a_dn, x_send, x_recv, e_send, e_recv, b_recv, b_up, b_dn,
    hm_send, hm_recv, hx_send, hf_recv, hf_send,
    c_local, c_send, c_recv, f_local, f_send, f_recv,
):
    t = lax.axis_index("tensor")
    d = lax.axis_index("dp")
    x, c = d // 2, d % 2
    mate = x * 2 + (1 - c)
    rows, width = og.shape
    tokens, hidden_width = gate.shape
    dev_cols = width // (2 * nx)
    part = dev_cols // PARTS
    a_cols = width // A_PIECES
    steps = hidden_width // tile
    half_blocks = nt // 2
    half_rows = half_blocks * rows
    near = max(1, half_blocks - 1)
    has_up, has_dn = t < nt - 1, t > 0
    inner = jnp.logical_and(has_up, has_dn)
    outer = jnp.logical_not(inner)

    def span(i, size):
        return pl.ds(pl.multiple_of(i * size, size), size)

    def remote(src, dst, send, recv, **where):
        return pltpu.make_async_remote_copy(
            src_ref=src, dst_ref=dst, send_sem=send, recv_sem=recv,
            device_id=where, device_id_type=MESH,
        )

    def other(j):
        return (x + j) % nx

    def far(j, core):
        return 2 * j + core

    barrier = pltpu.get_barrier_semaphore()

    @pl.when(has_up)
    def _():
        pl.semaphore_signal(barrier, 1, device_id={"tensor": t + 1}, device_id_type=MESH)

    @pl.when(has_dn)
    def _():
        pl.semaphore_signal(barrier, 1, device_id={"tensor": t - 1}, device_id_type=MESH)

    pl.semaphore_signal(barrier, 1, device_id={"dp": mate}, device_id_type=MESH)
    for j in range(1, nx):
        pl.semaphore_signal(barrier, 1, device_id={"dp": other(j) * 2 + c}, device_id_type=MESH)

    @pl.when(inner)
    def _():
        pl.semaphore_wait(barrier, nx + 2)

    @pl.when(outer)
    def _():
        pl.semaphore_wait(barrier, nx + 1)

    def a_copy(src, o, p, to, sems):
        return remote(src, og_v.at[o, :, span(p, a_cols)], sems.at[o, p], a_recv.at[o, p], tensor=to)

    def a_fwd(o, p, to, sems):
        return a_copy(og_v.at[o, :, span(p, a_cols)], o, p, to, sems)

    def a_event(e):
        k, p = e // A_PIECES + 1, e % A_PIECES

        @pl.when(t - k >= 0)
        def _():
            a_fwd(t - k, p, t + 1, a_up).wait_recv()

            @pl.when(has_up)
            def _():
                a_fwd(t - k, p, t + 1, a_up).start()

        @pl.when(t + k < nt)
        def _():
            a_fwd(t + k, p, t - 1, a_dn).wait_recv()

            @pl.when(has_dn)
            def _():
                a_fwd(t + k, p, t - 1, a_dn).start()

    def x_copy(j, k):
        xo = other(j)
        return remote(
            og.at[:, span(xo * 2 + k, dev_cols)], xb_v.at[nx - j - 1, t, k],
            x_send.at[j, k], x_recv.at[nx - j, k], dp=xo * 2 + c,
        )

    def x_arrived(j, k):
        return remote(xb_v.at[j - 1, t, k], xb_v.at[j - 1, t, k], x_send.at[j, k], x_recv.at[j, k], dp=mate)

    beside = jnp.where(has_up, t + 1, t - 1)
    last = PARTS - 1

    def e_copy(j, k):
        xo = other(j)
        return remote(
            og_v.at[beside, :, span((xo * 2 + k) * PARTS + last, part)],
            xb_v.at[nx - j - 1, beside, k, :, span(last, part)],
            e_send.at[j, k], e_recv.at[nx - j, k], dp=xo * 2 + c,
        )

    def e_arrived(j, k):
        ref = xb_v.at[j - 1, beside, k, :, span(last, part)]
        return remote(ref, ref, e_send.at[j, k], e_recv.at[j, k], dp=mate)

    def b_fwd(o, j, p, to, sems):
        ref = xb_v.at[j - 1, o, :, :, span(p, part)]
        return remote(ref, ref, sems.at[o, j, p], b_recv.at[o, j, p], tensor=to)

    def to_up(o, p):
        over_x = jnp.logical_and(jnp.logical_and(t + 1 == nt - 1, o == t), p == last)
        return jnp.logical_and(has_up, jnp.logical_not(over_x))

    def to_dn(o, p):
        over_x = jnp.logical_and(jnp.logical_and(t - 1 == 0, o == t), p == last)
        return jnp.logical_and(has_dn, jnp.logical_not(over_x))

    def b_own(p):
        for j in range(1, nx):
            @pl.when(to_up(t, p))
            def _():
                b_fwd(t, j, p, t + 1, b_up).start()

            @pl.when(to_dn(t, p))
            def _():
                b_fwd(t, j, p, t - 1, b_dn).start()

    def c_local_copy():
        return pltpu.make_async_copy(og_v.at[:, :, span(d, dev_cols)], cols_v.at[c], c_local)

    def c_mate():
        return remote(og_v.at[:, :, span(mate, dev_cols)], cols_v.at[c], c_send, c_recv, dp=mate)

    def f_local_copy(j, o, p):
        return pltpu.make_async_copy(
            xb_v.at[j - 1, o, c, :, span(p, part)], cols_v.at[far(j, c), o, :, span(p, part)],
            f_local.at[j, o, p],
        )

    def f_mate(j, o, p, core):
        return remote(
            xb_v.at[j - 1, o, 1 - c, :, span(p, part)], cols_v.at[far(j, core), o, :, span(p, part)],
            f_send.at[j, o, p], f_recv.at[far(j, core), o, p], dp=mate,
        )

    def share(j, o, p):
        f_local_copy(j, o, p).start()
        f_mate(j, o, p, c).start()

    def b_event(e, onward):
        p, k = e // (nt - 1), e % (nt - 1) + 1
        if onward:
            @pl.when(jnp.logical_and(inner, jnp.logical_and(k == 1, p > 0)))
            def _():
                b_own(p)
        over_x = jnp.logical_and(k == 1, p == last)
        for o, live, to, sems in (
            (t - k, t - k >= 0, t + 1, b_up),
            (t + k, t + k < nt, t - 1, b_dn),
        ):
            @pl.when(jnp.logical_and(live, inner if onward else outer))
            def _():
                for j in range(1, nx):
                    if onward:
                        b_fwd(o, j, p, to, sems).wait_recv()
                        b_fwd(o, j, p, to, sems).start()
                    else:
                        @pl.when(over_x)
                        def _():
                            for core in range(2):
                                e_arrived(j, core).wait_recv()

                        @pl.when(jnp.logical_not(over_x))
                        def _():
                            b_fwd(o, j, p, to, sems).wait_recv()
                    share(j, o, p)

    def h_far(i, j):
        return remote(
            hid_v.at[i, c], hid_v.at[i, far(nx - j, c)], hx_send.at[j, i], hf_recv.at[far(nx - j, c), i],
            dp=other(j) * 2 + c,
        )

    def h_mate(i):
        return remote(hid_v.at[i, c], hid_v.at[i, c], hm_send.at[i], hm_recv.at[i], dp=mate)

    def h_fwd(i, j, core):
        ref = hid_v.at[i, far(j, core)]
        return remote(ref, ref, hf_send.at[j, i], hf_recv.at[far(j, core), i], dp=mate)

    def h_event(i):
        for j in range(1, nx):
            h_fwd(i, j, c).wait_recv()
            h_fwd(i, j, c).start()

    own = pltpu.make_async_copy(og, og_v.at[t], own_sem)
    own.start()
    for p in range(A_PIECES):
        @pl.when(has_up)
        def _():
            a_copy(og.at[:, span(p, a_cols)], t, p, t + 1, a_up).start()

        @pl.when(has_dn)
        def _():
            a_copy(og.at[:, span(p, a_cols)], t, p, t - 1, a_dn).start()
    for j in range(1, nx):
        for k in range(2):
            x_copy(j, k).start()

    def hidden_step(gate_t, up_t):
        i = pl.program_id(0)
        g = gate_t[...].astype(jnp.float32)
        u = up_t[...].astype(jnp.float32)
        hid_v[i, c] = (g * jax.nn.sigmoid(g) * u).astype(jnp.bfloat16)
        for j in range(1, nx):
            h_far(i, j).start()
        h_mate(i).start()

    column_spec = pl.BlockSpec((tokens, tile), lambda i: (0, i))
    pltpu.emit_pipeline(hidden_step, grid=(steps,), in_specs=[column_spec, column_spec])(gate, up)

    @pl.loop(0, near * A_PIECES)
    def _(e):
        a_event(e)

    own.wait()

    @pl.when(outer)
    def _():
        for j in range(1, nx):
            for k in range(2):
                e_copy(j, k).start()
    for j in range(1, nx):
        for k in range(2):
            x_arrived(j, k).wait_recv()
        for p in range(PARTS):
            share(j, t, p)

    @pl.when(outer)
    def _():
        for p in range(PARTS):
            b_own(p)

    def spread(i, count, event, late=False):
        per_step = -(-count // steps)
        for n in range(per_step):
            e = i * per_step + n - ((steps * per_step - count) if late else 0)

            @pl.when(jnp.logical_and(e >= 0, e < count))
            def _():
                event(e)

    def gradient(half, events):
        blocks = pl.ds(half * half_blocks, half_blocks)
        lines = span(half, half_rows)

        def step(w_t, gate_t, up_t, gg_t, ug_t):
            block = og_v[blocks].reshape(half_rows, width)
            grad = lax.dot_general(
                block, w_t[...], (((1,), (1,)), ((), ())), preferred_element_type=jnp.float32
            )
            g = gate_t[...].astype(jnp.float32)
            u = up_t[...].astype(jnp.float32)
            sig = jax.nn.sigmoid(g)
            gg_t[...] = (grad * u * sig * (1.0 + g * (1.0 - sig))).astype(jnp.bfloat16)
            ug_t[...] = (grad * (g * sig)).astype(jnp.bfloat16)
            events(pl.program_id(0))

        spec = pl.BlockSpec((half_rows, tile), lambda i: (0, i))
        pltpu.emit_pipeline(
            step,
            grid=(steps,),
            in_specs=[pl.BlockSpec((tile, width), lambda i: (i, 0)), spec, spec],
            out_specs=[spec, spec],
        )(weight, gate.at[lines], up.at[lines], gate_grad.at[lines], up_grad.at[lines])

    h_third = max(1, steps // 7)
    h_second = 2 * h_third
    h_first = steps - h_second - h_third
    b_count = PARTS * (nt - 1)
    half = t // half_blocks

    a_next = (nt - 1 - near) * A_PIECES
    a_mid = min(a_next, A_PIECES)

    def first_events(i):
        spread(i, a_mid, lambda e: a_event(near * A_PIECES + e), late=True)

    gradient(half, first_events)

    @pl.loop(near * A_PIECES + a_mid, (nt - 1) * A_PIECES)
    def _(e):
        a_event(e)

    c_local_copy().start()
    c_mate().start()

    @pl.when(inner)
    def _():
        b_own(0)

    def second_events(i):
        def event(e):
            @pl.when(e < b_count)
            def _():
                b_event(e, True)

            @pl.when(e >= b_count)
            def _():
                h_event(e - b_count)

        spread(i, b_count + h_first, event)

    gradient(1 - half, second_events)

    @pl.loop(0, steps)
    def _(i):
        remote(hid_v.at[i, 1 - c], hid_v.at[i, 1 - c], hm_send.at[i], hm_recv.at[i], dp=mate).wait_recv()

    c_local_copy().wait()
    remote(og_v.at[:, :, span(mate, dev_cols)], cols_v.at[1 - c], c_send, c_recv, dp=mate).wait_recv()

    def product(i, lo, hi, cols):
        k = (hi - lo) * tokens
        return lax.dot_general(
            hid_v[i, lo:hi].reshape(k, tile), cols_v[lo:hi, :, :, cols].reshape(k, -1),
            (((0,), (0,)), ((), ())), preferred_element_type=jnp.float32,
        )

    @pl.loop(0, steps)
    def _(i):
        acc_v[span(i, tile), :] = product(i, 0, 2, slice(None))
        spread(i, h_second, lambda e: h_event(h_first + e), late=True)

    for p in range(PARTS):
        @pl.loop(p * (nt - 1), (p + 1) * (nt - 1))
        def _(e):
            b_event(e, False)

        for j in range(1, nx):
            @pl.loop(0, nt)
            def _(o):
                f_local_copy(j, o, p).wait()
                f_mate(j, o, p, 1 - c).wait_recv()

        def down_step(out_t):
            i = pl.program_id(0)
            if p == 0:
                @pl.when(i >= steps - 2 * h_third)
                def _():
                    e = i - (steps - 2 * h_third)

                    @pl.when(e < h_third)
                    def _():
                        h_event(steps - h_third + e)

                for j in range(1, nx):
                    h_fwd(i, j, 1 - c).wait_recv()
            cols = slice(p * part, (p + 1) * part)
            total = acc_v[span(i, tile), cols] + product(i, 2, 2 * nx, cols)
            out_t[...] = (total * scale).astype(jnp.bfloat16)

        pltpu.emit_pipeline(
            down_step,
            grid=(steps,),
            out_specs=[pl.BlockSpec((tile, part), lambda i: (i, p))],
        )(down_grad)

    c_mate().wait_send()
    for j in range(1, nx):
        for k in range(2):
            x_copy(j, k).wait_send()

            @pl.when(outer)
            def _():
                e_copy(j, k).wait_send()

        @pl.loop(0, nt)
        def _(o):
            for p in range(PARTS):
                f_mate(j, o, p, c).wait_send()

    @pl.loop(0, steps)
    def _(i):
        for j in range(1, nx):
            h_far(i, j).wait_send()
            h_fwd(i, j, c).wait_send()
        h_mate(i).wait_send()

    @pl.loop(0, nt)
    def _(o):
        @pl.when(jnp.logical_and(has_up, o <= t))
        def _():
            for p in range(A_PIECES):
                a_fwd(o, p, t + 1, a_up).wait_send()
            for p in range(PARTS):
                @pl.when(to_up(o, p))
                def _():
                    for j in range(1, nx):
                        b_fwd(o, j, p, t + 1, b_up).wait_send()

        @pl.when(jnp.logical_and(has_dn, o >= t))
        def _():
            for p in range(A_PIECES):
                a_fwd(o, p, t - 1, a_dn).wait_send()
            for p in range(PARTS):
                @pl.when(to_dn(o, p))
                def _():
                    for j in range(1, nx):
                        b_fwd(o, j, p, t - 1, b_dn).wait_send()


def on_device(out_grad, gate_pre, up_pre, down_weight):
    nt, dp = lax.axis_size("tensor"), lax.axis_size("dp")
    nx = dp // 2
    _, rows, width = out_grad.shape
    _, tokens, hidden_width = gate_pre.shape
    tile = 256 if hidden_width % 256 == 0 else 128
    steps = hidden_width // tile
    dev_cols = width // dp
    bf16 = jnp.bfloat16
    dma = pltpu.SemaphoreType.DMA
    any_spec = pl.BlockSpec(memory_space=pl.ANY)
    gate_grad, up_grad, down_grad = pl.pallas_call(
        functools.partial(exchange, nt, nx, tile, 1.0 / math.sqrt(tokens * dp)),
        out_shape=(
            jax.ShapeDtypeStruct((tokens, hidden_width), bf16),
            jax.ShapeDtypeStruct((tokens, hidden_width), bf16),
            jax.ShapeDtypeStruct((hidden_width, dev_cols), bf16),
        ),
        in_specs=[any_spec] * 4,
        out_specs=[any_spec] * 3,
        scratch_shapes=[
            pltpu.VMEM((nt, rows, width), bf16),
            pltpu.VMEM((nx - 1, nt, 2, rows, dev_cols), bf16),
            pltpu.VMEM((steps, 2 * nx, tokens, tile), bf16),
            pltpu.VMEM((2 * nx, nt, rows, dev_cols), bf16),
            pltpu.VMEM((hidden_width, dev_cols), jnp.float32),
            dma,
            dma((nt, A_PIECES)),
            dma((nt, A_PIECES)),
            dma((nt, A_PIECES)),
            dma((nx, 2)),
            dma((nx, 2)),
            dma((nx, 2)),
            dma((nx, 2)),
            dma((nt, nx, PARTS)),
            dma((nt, nx, PARTS)),
            dma((nt, nx, PARTS)),
            dma((steps,)),
            dma((steps,)),
            dma((nx, steps)),
            dma((2 * nx, steps)),
            dma((nx, steps)),
            dma,
            dma,
            dma,
            dma((nx, nt, PARTS)),
            dma((nx, nt, PARTS)),
            dma((2 * nx, nt, PARTS)),
        ],
        compiler_params=pltpu.CompilerParams(
            collective_id=0, has_side_effects=True, vmem_limit_bytes=60 * 2**20
        ),
    )(out_grad[0], gate_pre[0], up_pre[0], down_weight)
    return (gate_grad[None], up_grad[None], down_grad)


def solution(mesh):
    return jax.shard_map(
        on_device,
        mesh=mesh,
        in_specs=(
            P("dp", ("groups", "tensor"), None),
            P("dp", "groups", "tensor"),
            P("dp", "groups", "tensor"),
            P("tensor", None),
        ),
        out_specs=(
            P("dp", "groups", "tensor"),
            P("dp", "groups", "tensor"),
            P(("groups", "tensor"), "dp"),
        ),
        check_vma=False,
    )
```

```python
import functools
import math

import jax
import jax.numpy as jnp
from jax import lax
from jax.experimental import pallas as pl
from jax.experimental.pallas import tpu as pltpu
from jax.sharding import PartitionSpec as P

A_PIECES = 4
PARTS = 2
MESH = pl.DeviceIdType.MESH


def far_product(hid_v, cols_v, i, p):
    groups, tokens, chunk = hid_v.shape[1:]
    part = cols_v.shape[3] // PARTS
    k = groups * tokens
    return lax.dot_general(
        hid_v[i].reshape(k, chunk), cols_v[:, :, :, p * part:(p + 1) * part].reshape(k, part),
        (((0,), (0,)), ((), ())), preferred_element_type=jnp.float32,
    )


def finish(scale, gate_v, up_v, down_v, hid_v, cols_v, gate_grad, up_grad, down_grad, sems):
    steps, chunk = hid_v.shape[0], hid_v.shape[3]
    part = down_v.shape[1] // PARTS
    copies = [
        pltpu.make_async_copy(gate_v, gate_grad, sems.at[0]),
        pltpu.make_async_copy(up_v, up_grad, sems.at[1]),
        pltpu.make_async_copy(down_v.at[:, pl.ds(0, part)], down_grad.at[:, pl.ds(0, part)], sems.at[2]),
    ]
    for copy in copies:
        copy.start()

    def step(out_t):
        i = pl.program_id(0)
        lines = pl.ds(pl.multiple_of(i * chunk, chunk), chunk)
        total = down_v[lines, part:].astype(jnp.float32) + far_product(hid_v, cols_v, i, 1)
        out_t[...] = (total * scale).astype(jnp.bfloat16)

    pltpu.emit_pipeline(
        step, grid=(steps,), out_specs=[pl.BlockSpec((chunk, part), lambda i: (i, 1))]
    )(down_grad)
    for copy in copies:
        copy.wait()


def exchange(
    nt, nx, chunk, tile, scale,
    og, gate, up, weight,
    gate_grad, up_grad, down_v, hidf_v, colsf_v,
    og_v, xb_v, hid_v, cols_v,
    own_sem, a_recv, a_up, a_dn, x_send, x_recv, e_send, e_recv, b_recv, b_up, b_dn,
    hm_send, hm_recv, hx_send, hf_recv, hf_send,
    c_local, c_send, c_recv, f_local, f_send, f_recv,
):
    t = lax.axis_index("tensor")
    d = lax.axis_index("dp")
    x, c = d // 2, d % 2
    mate = x * 2 + (1 - c)
    rows, width = og.shape
    tokens, hidden_width = gate.shape
    dev_cols = width // (2 * nx)
    part = dev_cols // PARTS
    a_cols = width // A_PIECES
    steps = hidden_width // chunk
    tiles = hidden_width // tile
    half_blocks = nt // 2
    half_rows = half_blocks * rows
    near = max(1, half_blocks - 1)
    has_up, has_dn = t < nt - 1, t > 0
    inner = jnp.logical_and(has_up, has_dn)
    outer = jnp.logical_not(inner)

    def span(i, size):
        return pl.ds(pl.multiple_of(i * size, size), size)

    def remote(src, dst, send, recv, **where):
        return pltpu.make_async_remote_copy(
            src_ref=src, dst_ref=dst, send_sem=send, recv_sem=recv,
            device_id=where, device_id_type=MESH,
        )

    def other(j):
        return (x + j) % nx

    def far(j, core):
        return 2 * (j - 1) + core

    barrier = pltpu.get_barrier_semaphore()

    @pl.when(has_up)
    def _():
        pl.semaphore_signal(barrier, 1, device_id={"tensor": t + 1}, device_id_type=MESH)

    @pl.when(has_dn)
    def _():
        pl.semaphore_signal(barrier, 1, device_id={"tensor": t - 1}, device_id_type=MESH)

    pl.semaphore_signal(barrier, 1, device_id={"dp": mate}, device_id_type=MESH)
    for j in range(1, nx):
        pl.semaphore_signal(barrier, 1, device_id={"dp": other(j) * 2 + c}, device_id_type=MESH)

    @pl.when(inner)
    def _():
        pl.semaphore_wait(barrier, nx + 2)

    @pl.when(outer)
    def _():
        pl.semaphore_wait(barrier, nx + 1)

    def a_copy(src, o, p, to, sems):
        return remote(src, og_v.at[o, :, span(p, a_cols)], sems.at[o, p], a_recv.at[o, p], tensor=to)

    def a_fwd(o, p, to, sems):
        return a_copy(og_v.at[o, :, span(p, a_cols)], o, p, to, sems)

    def a_event(e):
        k, p = e // A_PIECES + 1, e % A_PIECES

        @pl.when(t - k >= 0)
        def _():
            a_fwd(t - k, p, t + 1, a_up).wait_recv()

            @pl.when(has_up)
            def _():
                a_fwd(t - k, p, t + 1, a_up).start()

        @pl.when(t + k < nt)
        def _():
            a_fwd(t + k, p, t - 1, a_dn).wait_recv()

            @pl.when(has_dn)
            def _():
                a_fwd(t + k, p, t - 1, a_dn).start()

    def x_copy(j, k):
        xo = other(j)
        return remote(
            og.at[:, span(xo * 2 + k, dev_cols)], xb_v.at[nx - j - 1, t, k],
            x_send.at[j, k], x_recv.at[nx - j, k], dp=xo * 2 + c,
        )

    def x_arrived(j, k):
        return remote(xb_v.at[j - 1, t, k], xb_v.at[j - 1, t, k], x_send.at[j, k], x_recv.at[j, k], dp=mate)

    beside = jnp.where(has_up, t + 1, t - 1)
    last = PARTS - 1

    def e_copy(j, k):
        xo = other(j)
        return remote(
            og_v.at[beside, :, span((xo * 2 + k) * PARTS + last, part)],
            xb_v.at[nx - j - 1, beside, k, :, span(last, part)],
            e_send.at[j, k], e_recv.at[nx - j, k], dp=xo * 2 + c,
        )

    def e_arrived(j, k):
        ref = xb_v.at[j - 1, beside, k, :, span(last, part)]
        return remote(ref, ref, e_send.at[j, k], e_recv.at[j, k], dp=mate)

    def b_fwd(o, j, p, to, sems):
        ref = xb_v.at[j - 1, o, :, :, span(p, part)]
        return remote(ref, ref, sems.at[o, j, p], b_recv.at[o, j, p], tensor=to)

    def to_up(o, p):
        over_x = jnp.logical_and(jnp.logical_and(t + 1 == nt - 1, o == t), p == last)
        return jnp.logical_and(has_up, jnp.logical_not(over_x))

    def to_dn(o, p):
        over_x = jnp.logical_and(jnp.logical_and(t - 1 == 0, o == t), p == last)
        return jnp.logical_and(has_dn, jnp.logical_not(over_x))

    def b_own(p):
        for j in range(1, nx):
            @pl.when(to_up(t, p))
            def _():
                b_fwd(t, j, p, t + 1, b_up).start()

            @pl.when(to_dn(t, p))
            def _():
                b_fwd(t, j, p, t - 1, b_dn).start()

    def blocks(h):
        return pl.ds(h * half_blocks, half_blocks)

    def c_local_copy(h):
        return pltpu.make_async_copy(
            og_v.at[blocks(h), :, span(d, dev_cols)], cols_v.at[c, blocks(h)], c_local.at[h]
        )

    def c_mate(h, core):
        return remote(
            og_v.at[blocks(h), :, span(mate, dev_cols)], cols_v.at[core, blocks(h)],
            c_send.at[h], c_recv.at[h], dp=mate,
        )

    def c_share(h):
        c_local_copy(h).start()
        c_mate(h, c).start()

    def c_wait(h):
        c_local_copy(h).wait()
        c_mate(h, 1 - c).wait_recv()

    def f_local_copy(j, o, p):
        return pltpu.make_async_copy(
            xb_v.at[j - 1, o, c, :, span(p, part)], colsf_v.at[far(j, c), o, :, span(p, part)],
            f_local.at[j, o, p],
        )

    def f_mate(j, o, p, core):
        return remote(
            xb_v.at[j - 1, o, 1 - c, :, span(p, part)], colsf_v.at[far(j, core), o, :, span(p, part)],
            f_send.at[j, o, p], f_recv.at[far(j, core), o, p], dp=mate,
        )

    def share(j, o, p):
        f_local_copy(j, o, p).start()
        f_mate(j, o, p, c).start()

    def b_event(e, onward):
        p, k = e // (nt - 1), e % (nt - 1) + 1
        if onward:
            @pl.when(jnp.logical_and(inner, jnp.logical_and(k == 1, p > 0)))
            def _():
                b_own(p)
        over_x = jnp.logical_and(k == 1, p == last)
        for o, live, to, sems in (
            (t - k, t - k >= 0, t + 1, b_up),
            (t + k, t + k < nt, t - 1, b_dn),
        ):
            @pl.when(jnp.logical_and(live, inner if onward else outer))
            def _():
                for j in range(1, nx):
                    if onward:
                        b_fwd(o, j, p, to, sems).wait_recv()
                        b_fwd(o, j, p, to, sems).start()
                    else:
                        @pl.when(over_x)
                        def _():
                            for core in range(2):
                                e_arrived(j, core).wait_recv()

                        @pl.when(jnp.logical_not(over_x))
                        def _():
                            b_fwd(o, j, p, to, sems).wait_recv()
                    share(j, o, p)

    def h_far(i, j):
        return remote(
            hid_v.at[i, c], hidf_v.at[i, far(nx - j, c)], hx_send.at[j, i], hf_recv.at[far(nx - j, c), i],
            dp=other(j) * 2 + c,
        )

    def h_mate(i):
        return remote(hid_v.at[i, c], hid_v.at[i, c], hm_send.at[i], hm_recv.at[i], dp=mate)

    def h_fwd(i, j, core):
        ref = hidf_v.at[i, far(j, core)]
        return remote(ref, ref, hf_send.at[j, i], hf_recv.at[far(j, core), i], dp=mate)

    def h_event(i):
        for j in range(1, nx):
            h_fwd(i, j, c).wait_recv()
            h_fwd(i, j, c).start()

    own = pltpu.make_async_copy(og, og_v.at[t], own_sem)
    own.start()
    for p in range(A_PIECES):
        @pl.when(has_up)
        def _():
            a_copy(og.at[:, span(p, a_cols)], t, p, t + 1, a_up).start()

        @pl.when(has_dn)
        def _():
            a_copy(og.at[:, span(p, a_cols)], t, p, t - 1, a_dn).start()
    for j in range(1, nx):
        for k in range(2):
            x_copy(j, k).start()

    def hidden_step(gate_t, up_t):
        i = pl.program_id(0)
        g = gate_t[...].astype(jnp.float32)
        u = up_t[...].astype(jnp.float32)
        hid_v[i, c] = (g * jax.nn.sigmoid(g) * u).astype(jnp.bfloat16)
        for j in range(1, nx):
            h_far(i, j).start()
        h_mate(i).start()

    column_spec = pl.BlockSpec((tokens, chunk), lambda i: (0, i))
    pltpu.emit_pipeline(hidden_step, grid=(steps,), in_specs=[column_spec, column_spec])(gate, up)

    def spread(i, total, count, event, late=False):
        per_step = -(-count // total)
        for n in range(per_step):
            e = i * per_step + n - ((total * per_step - count) if late else 0)

            @pl.when(jnp.logical_and(e >= 0, e < count))
            def _():
                event(e)

    h_third = max(1, steps // 7)
    h_second = 2 * h_third
    h_first = steps - h_second - h_third
    b_count = PARTS * (nt - 1)
    half = t // half_blocks
    a_count = (nt - 1) * A_PIECES
    a_near = near * A_PIECES
    a_mid = min(a_count - a_near, A_PIECES)

    def near_first():
        @pl.loop(0, a_near)
        def _(e):
            a_event(e)

        own.wait()
        c_share(half)

        @pl.when(outer)
        def _():
            for j in range(1, nx):
                for k in range(2):
                    e_copy(j, k).start()
        for j in range(1, nx):
            for k in range(2):
                x_arrived(j, k).wait_recv()
            for p in range(PARTS):
                share(j, t, p)

        @pl.when(outer)
        def _():
            for p in range(PARTS):
                b_own(p)

    def own_product(i, h):
        k = 2 * half_rows
        return lax.dot_general(
            hid_v[i, :, span(h, half_rows)].reshape(k, chunk), cols_v[:, blocks(h)].reshape(k, dev_cols),
            (((0,), (0,)), ((), ())), preferred_element_type=jnp.float32,
        )

    def far_first():
        c_wait(half)

        @pl.loop(0, steps)
        def _(i):
            remote(hid_v.at[i, 1 - c], hid_v.at[i, 1 - c], hm_send.at[i], hm_recv.at[i], dp=mate).wait_recv()
            down_v[span(i, chunk), :] = own_product(i, half).astype(jnp.bfloat16)
            spread(i, steps, a_mid, lambda e: a_event(a_near + e), late=True)

        @pl.loop(a_near + a_mid, a_count)
        def _(e):
            a_event(e)

        c_share(1 - half)

        @pl.when(inner)
        def _():
            b_own(0)

    def far_events(i):
        def event(e):
            @pl.when(e < b_count)
            def _():
                b_event(e, True)

            @pl.when(e >= b_count)
            def _():
                h_event(e - b_count)

        spread(i, tiles, b_count + h_first, event)

    def taken(b):
        return half + b * (1 - 2 * half)

    def gradient_step(w_t, gate_t, up_t):
        b, i = pl.program_id(0), pl.program_id(1)

        @pl.when(jnp.logical_and(b == 0, i == 0))
        def _():
            near_first()

        @pl.when(jnp.logical_and(b == 1, i == 0))
        def _():
            far_first()

        h = taken(b)
        block = og_v[blocks(h)].reshape(half_rows, width)
        grad = lax.dot_general(
            block, w_t[...], (((1,), (1,)), ((), ())), preferred_element_type=jnp.float32
        )
        g = gate_t[...].astype(jnp.float32)
        u = up_t[...].astype(jnp.float32)
        sig = jax.nn.sigmoid(g)
        out = (span(h, half_rows), span(i, tile))
        gate_grad[out] = (grad * u * sig * (1.0 + g * (1.0 - sig))).astype(jnp.bfloat16)
        up_grad[out] = (grad * (g * sig)).astype(jnp.bfloat16)

        @pl.when(b == 1)
        def _():
            far_events(i)

    deep = pl.Buffered(3)
    spec = pl.BlockSpec((half_rows, tile), lambda b, i: (taken(b), i), pipeline_mode=deep)
    pltpu.emit_pipeline(
        gradient_step,
        grid=(2, tiles),
        in_specs=[pl.BlockSpec((tile, width), lambda b, i: (i, 0), pipeline_mode=deep), spec, spec],
    )(weight, gate, up)
    c_wait(1 - half)

    @pl.loop(0, steps)
    def _(i):
        lines = span(i, chunk)
        down_v[lines, :] = (down_v[lines, :].astype(jnp.float32) + own_product(i, 1 - half)).astype(jnp.bfloat16)
        spread(i, steps, h_second, lambda e: h_event(h_first + e), late=True)

    def far_columns(p):
        @pl.loop(p * (nt - 1), (p + 1) * (nt - 1))
        def _(e):
            b_event(e, False)

        for j in range(1, nx):
            @pl.loop(0, nt)
            def _(o):
                f_local_copy(j, o, p).wait()
                f_mate(j, o, p, 1 - c).wait_recv()

    far_columns(0)

    @pl.loop(0, steps)
    def _(i):
        e = i - (steps - 2 * h_third)

        @pl.when(jnp.logical_and(e >= 0, e < h_third))
        def _():
            h_event(steps - h_third + e)

        for j in range(1, nx):
            h_fwd(i, j, 1 - c).wait_recv()
        lines = span(i, chunk)
        total = down_v[lines, 0:part].astype(jnp.float32) + far_product(hidf_v, colsf_v, i, 0)
        down_v[lines, 0:part] = (total * scale).astype(jnp.bfloat16)

    for p in range(1, PARTS):
        far_columns(p)

    for h in range(2):
        c_mate(h, c).wait_send()
    for j in range(1, nx):
        for k in range(2):
            x_copy(j, k).wait_send()

            @pl.when(outer)
            def _():
                e_copy(j, k).wait_send()

        @pl.loop(0, nt)
        def _(o):
            for p in range(PARTS):
                f_mate(j, o, p, c).wait_send()

    @pl.loop(0, steps)
    def _(i):
        for j in range(1, nx):
            h_far(i, j).wait_send()
            h_fwd(i, j, c).wait_send()
        h_mate(i).wait_send()

    @pl.loop(0, nt)
    def _(o):
        @pl.when(jnp.logical_and(has_up, o <= t))
        def _():
            for p in range(A_PIECES):
                a_fwd(o, p, t + 1, a_up).wait_send()
            for p in range(PARTS):
                @pl.when(to_up(o, p))
                def _():
                    for j in range(1, nx):
                        b_fwd(o, j, p, t + 1, b_up).wait_send()

        @pl.when(jnp.logical_and(has_dn, o >= t))
        def _():
            for p in range(A_PIECES):
                a_fwd(o, p, t - 1, a_dn).wait_send()
            for p in range(PARTS):
                @pl.when(to_dn(o, p))
                def _():
                    for j in range(1, nx):
                        b_fwd(o, j, p, t - 1, b_dn).wait_send()


def on_device(out_grad, gate_pre, up_pre, down_weight):
    nt, dp = lax.axis_size("tensor"), lax.axis_size("dp")
    nx = dp // 2
    _, rows, width = out_grad.shape
    _, tokens, hidden_width = gate_pre.shape
    chunk = next(n for n in (512, 256, 128) if hidden_width % n == 0)
    tile = min(chunk, 256)
    steps = hidden_width // chunk
    dev_cols = width // dp
    scale = 1.0 / math.sqrt(tokens * dp)
    bf16 = jnp.bfloat16
    dma = pltpu.SemaphoreType.DMA
    any_spec = pl.BlockSpec(memory_space=pl.ANY)
    vmem_spec = pl.BlockSpec(memory_space=pltpu.VMEM)
    kept = pl.pallas_call(
        functools.partial(exchange, nt, nx, chunk, tile, scale),
        out_shape=(
            pltpu.VMEM((tokens, hidden_width), bf16),
            pltpu.VMEM((tokens, hidden_width), bf16),
            pltpu.VMEM((hidden_width, dev_cols), bf16),
            pltpu.VMEM((steps, 2 * nx - 2, tokens, chunk), bf16),
            pltpu.VMEM((2 * nx - 2, nt, rows, dev_cols), bf16),
        ),
        in_specs=[any_spec] * 4,
        out_specs=[vmem_spec] * 5,
        scratch_shapes=[
            pltpu.VMEM((nt, rows, width), bf16),
            pltpu.VMEM((nx - 1, nt, 2, rows, dev_cols), bf16),
            pltpu.VMEM((steps, 2, tokens, chunk), bf16),
            pltpu.VMEM((2, nt, rows, dev_cols), bf16),
            dma,
            dma((nt, A_PIECES)),
            dma((nt, A_PIECES)),
            dma((nt, A_PIECES)),
            dma((nx, 2)),
            dma((nx, 2)),
            dma((nx, 2)),
            dma((nx, 2)),
            dma((nt, nx, PARTS)),
            dma((nt, nx, PARTS)),
            dma((nt, nx, PARTS)),
            dma((steps,)),
            dma((steps,)),
            dma((nx, steps)),
            dma((2 * nx, steps)),
            dma((nx, steps)),
            dma((2,)),
            dma((2,)),
            dma((2,)),
            dma((nx, nt, PARTS)),
            dma((nx, nt, PARTS)),
            dma((2 * nx, nt, PARTS)),
        ],
        compiler_params=pltpu.CompilerParams(
            collective_id=0, has_side_effects=True, vmem_limit_bytes=31 * 2**20
        ),
    )(out_grad[0], gate_pre[0], up_pre[0], down_weight)
    gate_grad, up_grad, down_grad = pl.pallas_call(
        functools.partial(finish, scale),
        out_shape=(
            jax.ShapeDtypeStruct((tokens, hidden_width), bf16),
            jax.ShapeDtypeStruct((tokens, hidden_width), bf16),
            jax.ShapeDtypeStruct((hidden_width, dev_cols), bf16),
        ),
        in_specs=[vmem_spec] * 5,
        out_specs=[any_spec] * 3,
        scratch_shapes=[dma((3,))],
        compiler_params=pltpu.CompilerParams(vmem_limit_bytes=8 * 2**20),
    )(*kept)
    return (gate_grad[None], up_grad[None], down_grad)


def solution(mesh):
    return jax.shard_map(
        on_device,
        mesh=mesh,
        in_specs=(
            P("dp", ("groups", "tensor"), None),
            P("dp", "groups", "tensor"),
            P("dp", "groups", "tensor"),
            P("tensor", None),
        ),
        out_specs=(
            P("dp", "groups", "tensor"),
            P("dp", "groups", "tensor"),
            P(("groups", "tensor"), "dp"),
        ),
        check_vma=False,
    )
```

```python
import functools
import math

import jax
import jax.numpy as jnp
from jax import lax
from jax.experimental import pallas as pl
from jax.experimental.pallas import tpu as pltpu
from jax.sharding import PartitionSpec as P

A_PIECES = 4
PARTS = 2
MESH = pl.DeviceIdType.MESH


def far_product(hid_v, cols_v, i, p):
    groups, tokens, chunk = hid_v.shape[1:]
    part = cols_v.shape[3] // PARTS
    k = groups * tokens
    return lax.dot_general(
        hid_v[i].reshape(k, chunk), cols_v[:, :, :, p * part:(p + 1) * part].reshape(k, part),
        (((0,), (0,)), ((), ())), preferred_element_type=jnp.float32,
    )


def finish(scale, gate_v, up_v, down_v, hid_v, cols_v, gate_grad, up_grad, down_grad, last_v, sems, last_sems):
    steps, chunk = hid_v.shape[0], hid_v.shape[3]
    part = down_v.shape[1] // PARTS
    copies = [
        pltpu.make_async_copy(gate_v, gate_grad, sems.at[0]),
        pltpu.make_async_copy(up_v, up_grad, sems.at[1]),
        pltpu.make_async_copy(down_v.at[:, pl.ds(0, part)], down_grad.at[:, pl.ds(0, part)], sems.at[2]),
    ]
    for copy in copies:
        copy.start()

    def last_copy(i):
        lines = pl.ds(i * chunk, chunk)
        return pltpu.make_async_copy(last_v.at[lines], down_grad.at[lines, pl.ds(part, part)], last_sems.at[i])

    for i in range(steps):
        lines = slice(i * chunk, (i + 1) * chunk)
        total = down_v[lines, part:].astype(jnp.float32) + far_product(hid_v, cols_v, i, 1)
        last_v[lines, :] = (total * scale).astype(jnp.bfloat16)
        last_copy(i).start()
    for i in range(steps):
        last_copy(i).wait()
    for copy in copies:
        copy.wait()


def exchange(
    nt, nx, chunk, tile, scale,
    og, gate, up, weight,
    gate_grad, up_grad, down_v, hidf_v, colsf_v,
    og_v, xb_v, hid_v, cols_v,
    own_sem, a_recv, a_up, a_dn, x_send, x_recv, e_send, e_recv, b_recv, b_up, b_dn,
    hm_send, hm_recv, hx_send, hf_recv, hf_send,
    c_local, c_send, c_recv, f_local, f_send, f_recv,
):
    t = lax.axis_index("tensor")
    d = lax.axis_index("dp")
    x, c = d // 2, d % 2
    mate = x * 2 + (1 - c)
    rows, width = og.shape
    tokens, hidden_width = gate.shape
    dev_cols = width // (2 * nx)
    part = dev_cols // PARTS
    a_cols = width // A_PIECES
    steps = hidden_width // chunk
    tiles = hidden_width // tile
    half_blocks = nt // 2
    half_rows = half_blocks * rows
    near = max(1, half_blocks - 1)
    has_up, has_dn = t < nt - 1, t > 0
    inner = jnp.logical_and(has_up, has_dn)
    outer = jnp.logical_not(inner)

    def span(i, size):
        return pl.ds(pl.multiple_of(i * size, size), size)

    def remote(src, dst, send, recv, **where):
        return pltpu.make_async_remote_copy(
            src_ref=src, dst_ref=dst, send_sem=send, recv_sem=recv,
            device_id=where, device_id_type=MESH,
        )

    def other(j):
        return (x + j) % nx

    def far(j, core):
        return 2 * (j - 1) + core

    barrier = pltpu.get_barrier_semaphore()

    @pl.when(has_up)
    def _():
        pl.semaphore_signal(barrier, 1, device_id={"tensor": t + 1}, device_id_type=MESH)

    @pl.when(has_dn)
    def _():
        pl.semaphore_signal(barrier, 1, device_id={"tensor": t - 1}, device_id_type=MESH)

    pl.semaphore_signal(barrier, 1, device_id={"dp": mate}, device_id_type=MESH)
    for j in range(1, nx):
        pl.semaphore_signal(barrier, 1, device_id={"dp": other(j) * 2 + c}, device_id_type=MESH)

    @pl.when(inner)
    def _():
        pl.semaphore_wait(barrier, nx + 2)

    @pl.when(outer)
    def _():
        pl.semaphore_wait(barrier, nx + 1)

    def a_copy(src, o, p, to, sems):
        return remote(src, og_v.at[o, :, span(p, a_cols)], sems.at[o, p], a_recv.at[o, p], tensor=to)

    def a_fwd(o, p, to, sems):
        return a_copy(og_v.at[o, :, span(p, a_cols)], o, p, to, sems)

    def a_event(e):
        k, p = e // A_PIECES + 1, e % A_PIECES

        @pl.when(t - k >= 0)
        def _():
            a_fwd(t - k, p, t + 1, a_up).wait_recv()

            @pl.when(has_up)
            def _():
                a_fwd(t - k, p, t + 1, a_up).start()

        @pl.when(t + k < nt)
        def _():
            a_fwd(t + k, p, t - 1, a_dn).wait_recv()

            @pl.when(has_dn)
            def _():
                a_fwd(t + k, p, t - 1, a_dn).start()

    def x_copy(j, k):
        xo = other(j)
        return remote(
            og.at[:, span(xo * 2 + k, dev_cols)], xb_v.at[nx - j - 1, t, k],
            x_send.at[j, k], x_recv.at[nx - j, k], dp=xo * 2 + c,
        )

    def x_arrived(j, k):
        return remote(xb_v.at[j - 1, t, k], xb_v.at[j - 1, t, k], x_send.at[j, k], x_recv.at[j, k], dp=mate)

    beside = jnp.where(has_up, t + 1, t - 1)
    last = PARTS - 1

    def e_copy(j, k):
        xo = other(j)
        return remote(
            og_v.at[beside, :, span((xo * 2 + k) * PARTS + last, part)],
            xb_v.at[nx - j - 1, beside, k, :, span(last, part)],
            e_send.at[j, k], e_recv.at[nx - j, k], dp=xo * 2 + c,
        )

    def e_arrived(j, k):
        ref = xb_v.at[j - 1, beside, k, :, span(last, part)]
        return remote(ref, ref, e_send.at[j, k], e_recv.at[j, k], dp=mate)

    def b_fwd(o, j, p, to, sems):
        ref = xb_v.at[j - 1, o, :, :, span(p, part)]
        return remote(ref, ref, sems.at[o, j, p], b_recv.at[o, j, p], tensor=to)

    def to_up(o, p):
        over_x = jnp.logical_and(jnp.logical_and(t + 1 == nt - 1, o == t), p == last)
        return jnp.logical_and(has_up, jnp.logical_not(over_x))

    def to_dn(o, p):
        over_x = jnp.logical_and(jnp.logical_and(t - 1 == 0, o == t), p == last)
        return jnp.logical_and(has_dn, jnp.logical_not(over_x))

    def b_own(p):
        for j in range(1, nx):
            @pl.when(to_up(t, p))
            def _():
                b_fwd(t, j, p, t + 1, b_up).start()

            @pl.when(to_dn(t, p))
            def _():
                b_fwd(t, j, p, t - 1, b_dn).start()

    def blocks(h):
        return pl.ds(h * half_blocks, half_blocks)

    def c_local_copy(h):
        return pltpu.make_async_copy(
            og_v.at[blocks(h), :, span(d, dev_cols)], cols_v.at[c, blocks(h)], c_local.at[h]
        )

    def c_mate(h, core):
        return remote(
            og_v.at[blocks(h), :, span(mate, dev_cols)], cols_v.at[core, blocks(h)],
            c_send.at[h], c_recv.at[h], dp=mate,
        )

    def c_share(h):
        c_local_copy(h).start()
        c_mate(h, c).start()

    def c_wait(h):
        c_local_copy(h).wait()
        c_mate(h, 1 - c).wait_recv()

    def f_local_copy(j, o, p):
        return pltpu.make_async_copy(
            xb_v.at[j - 1, o, c, :, span(p, part)], colsf_v.at[far(j, c), o, :, span(p, part)],
            f_local.at[j, o, p],
        )

    def f_mate(j, o, p, core):
        return remote(
            xb_v.at[j - 1, o, 1 - c, :, span(p, part)], colsf_v.at[far(j, core), o, :, span(p, part)],
            f_send.at[j, o, p], f_recv.at[far(j, core), o, p], dp=mate,
        )

    def share(j, o, p):
        f_local_copy(j, o, p).start()
        f_mate(j, o, p, c).start()

    def b_event(e, onward):
        p, k = e // (nt - 1), e % (nt - 1) + 1
        if onward:
            @pl.when(jnp.logical_and(inner, jnp.logical_and(k == 1, p > 0)))
            def _():
                b_own(p)
        over_x = jnp.logical_and(k == 1, p == last)
        for o, live, to, sems in (
            (t - k, t - k >= 0, t + 1, b_up),
            (t + k, t + k < nt, t - 1, b_dn),
        ):
            @pl.when(jnp.logical_and(live, inner if onward else outer))
            def _():
                for j in range(1, nx):
                    if onward:
                        b_fwd(o, j, p, to, sems).wait_recv()
                        b_fwd(o, j, p, to, sems).start()
                    else:
                        @pl.when(over_x)
                        def _():
                            for core in range(2):
                                e_arrived(j, core).wait_recv()

                        @pl.when(jnp.logical_not(over_x))
                        def _():
                            b_fwd(o, j, p, to, sems).wait_recv()
                    share(j, o, p)

    def h_far(i, j):
        return remote(
            hid_v.at[i, c], hidf_v.at[i, far(nx - j, c)], hx_send.at[j, i], hf_recv.at[far(nx - j, c), i],
            dp=other(j) * 2 + c,
        )

    def h_mate(i):
        return remote(hid_v.at[i, c], hid_v.at[i, c], hm_send.at[i], hm_recv.at[i], dp=mate)

    def h_fwd(i, j, core):
        ref = hidf_v.at[i, far(j, core)]
        return remote(ref, ref, hf_send.at[j, i], hf_recv.at[far(j, core), i], dp=mate)

    def h_event(i):
        for j in range(1, nx):
            h_fwd(i, j, c).wait_recv()
            h_fwd(i, j, c).start()

    own = pltpu.make_async_copy(og, og_v.at[t], own_sem)
    own.start()
    for p in range(A_PIECES):
        @pl.when(has_up)
        def _():
            a_copy(og.at[:, span(p, a_cols)], t, p, t + 1, a_up).start()

        @pl.when(has_dn)
        def _():
            a_copy(og.at[:, span(p, a_cols)], t, p, t - 1, a_dn).start()
    for j in range(1, nx):
        for k in range(2):
            x_copy(j, k).start()

    def hidden_step(gate_t, up_t):
        i = pl.program_id(0)
        g = gate_t[...].astype(jnp.float32)
        u = up_t[...].astype(jnp.float32)
        hid_v[i, c] = (g * jax.nn.sigmoid(g) * u).astype(jnp.bfloat16)
        for j in range(1, nx):
            h_far(i, j).start()
        h_mate(i).start()

    column_spec = pl.BlockSpec((tokens, chunk), lambda i: (0, i))
    pltpu.emit_pipeline(hidden_step, grid=(steps,), in_specs=[column_spec, column_spec])(gate, up)

    def spread(i, total, count, event, late=False):
        per_step = -(-count // total)
        for n in range(per_step):
            e = i * per_step + n - ((total * per_step - count) if late else 0)

            @pl.when(jnp.logical_and(e >= 0, e < count))
            def _():
                event(e)

    h_third = max(1, steps // 7)
    h_second = 2 * h_third
    h_first = steps - h_second - h_third
    b_count = PARTS * (nt - 1)
    half = t // half_blocks
    a_count = (nt - 1) * A_PIECES
    a_near = near * A_PIECES
    a_mid = min(a_count - a_near, A_PIECES)

    def near_first():
        @pl.loop(0, a_near)
        def _(e):
            a_event(e)

        own.wait()
        c_share(half)

        @pl.when(outer)
        def _():
            for j in range(1, nx):
                for k in range(2):
                    e_copy(j, k).start()
        for j in range(1, nx):
            for k in range(2):
                x_arrived(j, k).wait_recv()
            for p in range(PARTS):
                share(j, t, p)

        @pl.when(outer)
        def _():
            for p in range(PARTS):
                b_own(p)

    def own_product(i, h):
        k = 2 * half_rows
        return lax.dot_general(
            hid_v[i, :, span(h, half_rows)].reshape(k, chunk), cols_v[:, blocks(h)].reshape(k, dev_cols),
            (((0,), (0,)), ((), ())), preferred_element_type=jnp.float32,
        )

    def far_first():
        c_wait(half)

        @pl.loop(0, steps)
        def _(i):
            remote(hid_v.at[i, 1 - c], hid_v.at[i, 1 - c], hm_send.at[i], hm_recv.at[i], dp=mate).wait_recv()
            down_v[span(i, chunk), :] = own_product(i, half).astype(jnp.bfloat16)
            spread(i, steps, a_mid, lambda e: a_event(a_near + e), late=True)

        @pl.loop(a_near + a_mid, a_count)
        def _(e):
            a_event(e)

        c_share(1 - half)

        @pl.when(inner)
        def _():
            b_own(0)

    def far_events(i):
        def event(e):
            @pl.when(e < b_count)
            def _():
                b_event(e, True)

            @pl.when(e >= b_count)
            def _():
                h_event(e - b_count)

        spread(i, tiles, b_count + h_first, event)

    def taken(b):
        return half + b * (1 - 2 * half)

    def gradient_step(w_t, gate_t, up_t):
        b, i = pl.program_id(0), pl.program_id(1)

        @pl.when(jnp.logical_and(b == 0, i == 0))
        def _():
            near_first()

        @pl.when(jnp.logical_and(b == 1, i == 0))
        def _():
            far_first()

        h = taken(b)
        block = og_v[blocks(h)].reshape(half_rows, width)
        grad = lax.dot_general(
            block, w_t[...], (((1,), (1,)), ((), ())), preferred_element_type=jnp.float32
        )
        g = gate_t[...].astype(jnp.float32)
        u = up_t[...].astype(jnp.float32)
        sig = jax.nn.sigmoid(g)
        out = (span(h, half_rows), span(i, tile))
        gate_grad[out] = (grad * u * sig * (1.0 + g * (1.0 - sig))).astype(jnp.bfloat16)
        up_grad[out] = (grad * (g * sig)).astype(jnp.bfloat16)

        @pl.when(b == 1)
        def _():
            far_events(i)

    deep = pl.Buffered(3)
    spec = pl.BlockSpec((half_rows, tile), lambda b, i: (taken(b), i), pipeline_mode=deep)
    pltpu.emit_pipeline(
        gradient_step,
        grid=(2, tiles),
        in_specs=[pl.BlockSpec((tile, width), lambda b, i: (i, 0), pipeline_mode=deep), spec, spec],
    )(weight, gate, up)
    c_wait(1 - half)

    @pl.loop(0, steps)
    def _(i):
        lines = span(i, chunk)
        down_v[lines, :] = (down_v[lines, :].astype(jnp.float32) + own_product(i, 1 - half)).astype(jnp.bfloat16)
        spread(i, steps, h_second, lambda e: h_event(h_first + e), late=True)

    def far_columns(p):
        @pl.loop(p * (nt - 1), (p + 1) * (nt - 1))
        def _(e):
            b_event(e, False)

        for j in range(1, nx):
            @pl.loop(0, nt)
            def _(o):
                f_local_copy(j, o, p).wait()
                f_mate(j, o, p, 1 - c).wait_recv()

    far_columns(0)

    @pl.loop(0, steps)
    def _(i):
        e = i - (steps - 2 * h_third)

        @pl.when(jnp.logical_and(e >= 0, e < h_third))
        def _():
            h_event(steps - h_third + e)

        for j in range(1, nx):
            h_fwd(i, j, 1 - c).wait_recv()
        lines = span(i, chunk)
        total = down_v[lines, 0:part].astype(jnp.float32) + far_product(hidf_v, colsf_v, i, 0)
        down_v[lines, 0:part] = (total * scale).astype(jnp.bfloat16)

    for p in range(1, PARTS):
        far_columns(p)

    for h in range(2):
        c_mate(h, c).wait_send()
    for j in range(1, nx):
        for k in range(2):
            x_copy(j, k).wait_send()

            @pl.when(outer)
            def _():
                e_copy(j, k).wait_send()

        @pl.loop(0, nt)
        def _(o):
            for p in range(PARTS):
                f_mate(j, o, p, c).wait_send()

    @pl.loop(0, steps)
    def _(i):
        for j in range(1, nx):
            h_far(i, j).wait_send()
            h_fwd(i, j, c).wait_send()
        h_mate(i).wait_send()

    @pl.loop(0, nt)
    def _(o):
        @pl.when(jnp.logical_and(has_up, o <= t))
        def _():
            for p in range(A_PIECES):
                a_fwd(o, p, t + 1, a_up).wait_send()
            for p in range(PARTS):
                @pl.when(to_up(o, p))
                def _():
                    for j in range(1, nx):
                        b_fwd(o, j, p, t + 1, b_up).wait_send()

        @pl.when(jnp.logical_and(has_dn, o >= t))
        def _():
            for p in range(A_PIECES):
                a_fwd(o, p, t - 1, a_dn).wait_send()
            for p in range(PARTS):
                @pl.when(to_dn(o, p))
                def _():
                    for j in range(1, nx):
                        b_fwd(o, j, p, t - 1, b_dn).wait_send()


def on_device(out_grad, gate_pre, up_pre, down_weight):
    nt, dp = lax.axis_size("tensor"), lax.axis_size("dp")
    nx = dp // 2
    _, rows, width = out_grad.shape
    _, tokens, hidden_width = gate_pre.shape
    chunk = next(n for n in (512, 256, 128) if hidden_width % n == 0)
    tile = min(chunk, 256)
    steps = hidden_width // chunk
    dev_cols = width // dp
    scale = 1.0 / math.sqrt(tokens * dp)
    bf16 = jnp.bfloat16
    dma = pltpu.SemaphoreType.DMA
    any_spec = pl.BlockSpec(memory_space=pl.ANY)
    vmem_spec = pl.BlockSpec(memory_space=pltpu.VMEM)
    kept = pl.pallas_call(
        functools.partial(exchange, nt, nx, chunk, tile, scale),
        out_shape=(
            pltpu.VMEM((tokens, hidden_width), bf16),
            pltpu.VMEM((tokens, hidden_width), bf16),
            pltpu.VMEM((hidden_width, dev_cols), bf16),
            pltpu.VMEM((steps, 2 * nx - 2, tokens, chunk), bf16),
            pltpu.VMEM((2 * nx - 2, nt, rows, dev_cols), bf16),
        ),
        in_specs=[any_spec] * 4,
        out_specs=[vmem_spec] * 5,
        scratch_shapes=[
            pltpu.VMEM((nt, rows, width), bf16),
            pltpu.VMEM((nx - 1, nt, 2, rows, dev_cols), bf16),
            pltpu.VMEM((steps, 2, tokens, chunk), bf16),
            pltpu.VMEM((2, nt, rows, dev_cols), bf16),
            dma,
            dma((nt, A_PIECES)),
            dma((nt, A_PIECES)),
            dma((nt, A_PIECES)),
            dma((nx, 2)),
            dma((nx, 2)),
            dma((nx, 2)),
            dma((nx, 2)),
            dma((nt, nx, PARTS)),
            dma((nt, nx, PARTS)),
            dma((nt, nx, PARTS)),
            dma((steps,)),
            dma((steps,)),
            dma((nx, steps)),
            dma((2 * nx, steps)),
            dma((nx, steps)),
            dma((2,)),
            dma((2,)),
            dma((2,)),
            dma((nx, nt, PARTS)),
            dma((nx, nt, PARTS)),
            dma((2 * nx, nt, PARTS)),
        ],
        compiler_params=pltpu.CompilerParams(
            collective_id=0, has_side_effects=True, vmem_limit_bytes=31 * 2**20
        ),
    )(out_grad[0], gate_pre[0], up_pre[0], down_weight)
    gate_grad, up_grad, down_grad = pl.pallas_call(
        functools.partial(finish, scale),
        out_shape=(
            jax.ShapeDtypeStruct((tokens, hidden_width), bf16),
            jax.ShapeDtypeStruct((tokens, hidden_width), bf16),
            jax.ShapeDtypeStruct((hidden_width, dev_cols), bf16),
        ),
        in_specs=[vmem_spec] * 5,
        out_specs=[any_spec] * 3,
        scratch_shapes=[pltpu.VMEM((hidden_width, dev_cols // PARTS), bf16), dma((3,)), dma((steps,))],
        compiler_params=pltpu.CompilerParams(vmem_limit_bytes=8 * 2**20),
    )(*kept)
    return (gate_grad[None], up_grad[None], down_grad)


def solution(mesh):
    return jax.shard_map(
        on_device,
        mesh=mesh,
        in_specs=(
            P("dp", ("groups", "tensor"), None),
            P("dp", "groups", "tensor"),
            P("dp", "groups", "tensor"),
            P("tensor", None),
        ),
        out_specs=(
            P("dp", "groups", "tensor"),
            P("dp", "groups", "tensor"),
            P(("groups", "tensor"), "dp"),
        ),
        check_vma=False,
    )
```

```python
import functools
import math

import jax
import jax.numpy as jnp
from jax import lax
from jax.experimental import pallas as pl
from jax.experimental.pallas import tpu as pltpu
from jax.sharding import PartitionSpec as P

A_PIECES = 4
PARTS = 2
MESH = pl.DeviceIdType.MESH


def far_product(hid_v, cols_v, i, p):
    groups, tokens, chunk = hid_v.shape[1:]
    part = cols_v.shape[3] // PARTS
    k = groups * tokens
    return lax.dot_general(
        hid_v[i].reshape(k, chunk), cols_v[:, :, :, p * part:(p + 1) * part].reshape(k, part),
        (((0,), (0,)), ((), ())), preferred_element_type=jnp.float32,
    )


def finish(scale, gate_v, up_v, down_v, hid_v, cols_v, gate_grad, up_grad, down_grad, last_v, sems, last_sems):
    steps, chunk = hid_v.shape[0], hid_v.shape[3]
    part = down_v.shape[1] // PARTS
    copies = [
        pltpu.make_async_copy(gate_v, gate_grad, sems.at[0]),
        pltpu.make_async_copy(up_v, up_grad, sems.at[1]),
        pltpu.make_async_copy(down_v.at[:, pl.ds(0, part)], down_grad.at[:, pl.ds(0, part)], sems.at[2]),
    ]
    for copy in copies:
        copy.start()

    def last_copy(i):
        lines = pl.ds(i * chunk, chunk)
        return pltpu.make_async_copy(last_v.at[lines], down_grad.at[lines, pl.ds(part, part)], last_sems.at[i])

    for i in range(steps):
        lines = slice(i * chunk, (i + 1) * chunk)
        total = down_v[lines, part:].astype(jnp.float32) + far_product(hid_v, cols_v, i, 1)
        last_v[lines, :] = (total * scale).astype(jnp.bfloat16)
        last_copy(i).start()
    for i in range(steps):
        last_copy(i).wait()
    for copy in copies:
        copy.wait()


def exchange(
    nt, nx, chunk, tile, scale,
    og, gate, up, weight,
    gate_grad, up_grad, down_v, hidf_v, colsf_v,
    og_v, hid_v, cols_v,
    own_sem, a_recv, a_up, a_dn, x_send, x_recv, e_send, e_recv, b_recv, b_up, b_dn,
    hm_send, hm_recv, hx_send, hf_recv, hf_send,
    c_local, c_send, c_recv,
):
    t = lax.axis_index("tensor")
    d = lax.axis_index("dp")
    x, c = d // 2, d % 2
    mate = x * 2 + (1 - c)
    rows, width = og.shape
    tokens, hidden_width = gate.shape
    dev_cols = width // (2 * nx)
    part = dev_cols // PARTS
    a_cols = width // A_PIECES
    steps = hidden_width // chunk
    tiles = hidden_width // tile
    half_blocks = nt // 2
    half_rows = half_blocks * rows
    near = max(1, half_blocks - 1)
    has_up, has_dn = t < nt - 1, t > 0
    inner = jnp.logical_and(has_up, has_dn)
    outer = jnp.logical_not(inner)

    def span(i, size):
        return pl.ds(pl.multiple_of(i * size, size), size)

    def remote(src, dst, send, recv, **where):
        return pltpu.make_async_remote_copy(
            src_ref=src, dst_ref=dst, send_sem=send, recv_sem=recv,
            device_id=where, device_id_type=MESH,
        )

    def other(j):
        return (x + j) % nx

    def far(j, core):
        return 2 * (j - 1) + core

    barrier = pltpu.get_barrier_semaphore()

    @pl.when(has_up)
    def _():
        pl.semaphore_signal(barrier, 1, device_id={"tensor": t + 1}, device_id_type=MESH)

    @pl.when(has_dn)
    def _():
        pl.semaphore_signal(barrier, 1, device_id={"tensor": t - 1}, device_id_type=MESH)

    pl.semaphore_signal(barrier, 1, device_id={"dp": mate}, device_id_type=MESH)
    for j in range(1, nx):
        for k in range(2):
            pl.semaphore_signal(barrier, 1, device_id={"dp": other(j) * 2 + k}, device_id_type=MESH)

    @pl.when(inner)
    def _():
        pl.semaphore_wait(barrier, 2 * nx + 1)

    @pl.when(outer)
    def _():
        pl.semaphore_wait(barrier, 2 * nx)

    def a_copy(src, o, p, to, sems):
        return remote(src, og_v.at[o, :, span(p, a_cols)], sems.at[o, p], a_recv.at[o, p], tensor=to)

    def a_fwd(o, p, to, sems):
        return a_copy(og_v.at[o, :, span(p, a_cols)], o, p, to, sems)

    def a_event(e):
        k, p = e // A_PIECES + 1, e % A_PIECES

        @pl.when(t - k >= 0)
        def _():
            a_fwd(t - k, p, t + 1, a_up).wait_recv()

            @pl.when(has_up)
            def _():
                a_fwd(t - k, p, t + 1, a_up).start()

        @pl.when(t + k < nt)
        def _():
            a_fwd(t + k, p, t - 1, a_dn).wait_recv()

            @pl.when(has_dn)
            def _():
                a_fwd(t + k, p, t - 1, a_dn).start()

    def x_copy(j, k):
        xo = other(j)
        slot = far(nx - j, c)
        return remote(
            og.at[:, span(xo * 2 + k, dev_cols)], colsf_v.at[slot, t],
            x_send.at[j, k], x_recv.at[slot], dp=xo * 2 + k,
        )

    def x_arrived(j, core):
        ref = colsf_v.at[far(j, core), t]
        return remote(ref, ref, x_send.at[j, core], x_recv.at[far(j, core)], dp=mate)

    beside = jnp.where(has_up, t + 1, t - 1)
    last = PARTS - 1

    def e_copy(j, k):
        xo = other(j)
        slot = far(nx - j, c)
        return remote(
            og_v.at[beside, :, span((xo * 2 + k) * PARTS + last, part)],
            colsf_v.at[slot, beside, :, span(last, part)],
            e_send.at[j, k], e_recv.at[slot], dp=xo * 2 + k,
        )

    def e_arrived(j, core):
        ref = colsf_v.at[far(j, core), beside, :, span(last, part)]
        return remote(ref, ref, e_send.at[j, core], e_recv.at[far(j, core)], dp=mate)

    def b_fwd(o, j, p, to, sems):
        ref = colsf_v.at[pl.ds(far(j, 0), 2), o, :, span(p, part)]
        return remote(ref, ref, sems.at[o, j, p], b_recv.at[o, j, p], tensor=to)

    def to_up(o, p):
        over_x = jnp.logical_and(jnp.logical_and(t + 1 == nt - 1, o == t), p == last)
        return jnp.logical_and(has_up, jnp.logical_not(over_x))

    def to_dn(o, p):
        over_x = jnp.logical_and(jnp.logical_and(t - 1 == 0, o == t), p == last)
        return jnp.logical_and(has_dn, jnp.logical_not(over_x))

    def b_own(p):
        for j in range(1, nx):
            @pl.when(to_up(t, p))
            def _():
                b_fwd(t, j, p, t + 1, b_up).start()

            @pl.when(to_dn(t, p))
            def _():
                b_fwd(t, j, p, t - 1, b_dn).start()

    def blocks(h):
        return pl.ds(h * half_blocks, half_blocks)

    def c_local_copy(h):
        return pltpu.make_async_copy(
            og_v.at[blocks(h), :, span(d, dev_cols)], cols_v.at[c, blocks(h)], c_local.at[h]
        )

    def c_mate(h, core):
        return remote(
            og_v.at[blocks(h), :, span(mate, dev_cols)], cols_v.at[core, blocks(h)],
            c_send.at[h], c_recv.at[h], dp=mate,
        )

    def c_share(h):
        c_local_copy(h).start()
        c_mate(h, c).start()

    def c_wait(h):
        c_local_copy(h).wait()
        c_mate(h, 1 - c).wait_recv()

    def b_event(e, onward):
        p, k = e // (nt - 1), e % (nt - 1) + 1
        if onward:
            @pl.when(jnp.logical_and(inner, jnp.logical_and(k == 1, p > 0)))
            def _():
                b_own(p)
        over_x = jnp.logical_and(k == 1, p == last)
        for o, live, to, sems in (
            (t - k, t - k >= 0, t + 1, b_up),
            (t + k, t + k < nt, t - 1, b_dn),
        ):
            @pl.when(jnp.logical_and(live, inner if onward else outer))
            def _():
                for j in range(1, nx):
                    if onward:
                        b_fwd(o, j, p, to, sems).wait_recv()
                        b_fwd(o, j, p, to, sems).start()
                    else:
                        @pl.when(over_x)
                        def _():
                            for core in range(2):
                                e_arrived(j, core).wait_recv()

                        @pl.when(jnp.logical_not(over_x))
                        def _():
                            b_fwd(o, j, p, to, sems).wait_recv()

    def h_far(i, j):
        return remote(
            hid_v.at[i, c], hidf_v.at[i, far(nx - j, c)], hx_send.at[j, i], hf_recv.at[far(nx - j, c), i],
            dp=other(j) * 2 + c,
        )

    def h_mate(i):
        return remote(hid_v.at[i, c], hid_v.at[i, c], hm_send.at[i], hm_recv.at[i], dp=mate)

    def h_fwd(i, j, core):
        ref = hidf_v.at[i, far(j, core)]
        return remote(ref, ref, hf_send.at[j, i], hf_recv.at[far(j, core), i], dp=mate)

    def h_event(i):
        for j in range(1, nx):
            h_fwd(i, j, c).wait_recv()
            h_fwd(i, j, c).start()

    own = pltpu.make_async_copy(og, og_v.at[t], own_sem)
    own.start()
    for p in range(A_PIECES):
        @pl.when(has_up)
        def _():
            a_copy(og.at[:, span(p, a_cols)], t, p, t + 1, a_up).start()

        @pl.when(has_dn)
        def _():
            a_copy(og.at[:, span(p, a_cols)], t, p, t - 1, a_dn).start()
    for j in range(1, nx):
        for k in range(2):
            x_copy(j, k).start()

    def hidden_step(gate_t, up_t):
        i = pl.program_id(0)
        g = gate_t[...].astype(jnp.float32)
        u = up_t[...].astype(jnp.float32)
        hid_v[i, c] = (g * jax.nn.sigmoid(g) * u).astype(jnp.bfloat16)
        for j in range(1, nx):
            h_far(i, j).start()
        h_mate(i).start()

    column_spec = pl.BlockSpec((tokens, chunk), lambda i: (0, i))
    pltpu.emit_pipeline(hidden_step, grid=(steps,), in_specs=[column_spec, column_spec])(gate, up)

    def spread(i, total, count, event, late=False):
        per_step = -(-count // total)
        for n in range(per_step):
            e = i * per_step + n - ((total * per_step - count) if late else 0)

            @pl.when(jnp.logical_and(e >= 0, e < count))
            def _():
                event(e)

    h_third = max(1, steps // 7)
    h_second = 2 * h_third
    h_first = steps - h_second - h_third
    b_count = PARTS * (nt - 1)
    half = t // half_blocks
    a_count = (nt - 1) * A_PIECES
    a_near = near * A_PIECES
    a_mid = min(a_count - a_near, A_PIECES)

    def near_first():
        @pl.loop(0, a_near)
        def _(e):
            a_event(e)

        own.wait()
        c_share(half)

        @pl.when(outer)
        def _():
            for j in range(1, nx):
                for k in range(2):
                    e_copy(j, k).start()
        for j in range(1, nx):
            for k in range(2):
                x_arrived(j, k).wait_recv()

        @pl.when(outer)
        def _():
            for p in range(PARTS):
                b_own(p)

    def own_product(i, h):
        k = 2 * half_rows
        return lax.dot_general(
            hid_v[i, :, span(h, half_rows)].reshape(k, chunk), cols_v[:, blocks(h)].reshape(k, dev_cols),
            (((0,), (0,)), ((), ())), preferred_element_type=jnp.float32,
        )

    def far_first():
        c_wait(half)

        @pl.loop(0, steps)
        def _(i):
            remote(hid_v.at[i, 1 - c], hid_v.at[i, 1 - c], hm_send.at[i], hm_recv.at[i], dp=mate).wait_recv()
            down_v[span(i, chunk), :] = own_product(i, half).astype(jnp.bfloat16)
            spread(i, steps, a_mid, lambda e: a_event(a_near + e), late=True)

        @pl.loop(a_near + a_mid, a_count)
        def _(e):
            a_event(e)

        c_share(1 - half)

        @pl.when(inner)
        def _():
            b_own(0)

    def far_events(i):
        def event(e):
            @pl.when(e < b_count)
            def _():
                b_event(e, True)

            @pl.when(e >= b_count)
            def _():
                h_event(e - b_count)

        spread(i, tiles, b_count + h_first, event)

    def taken(b):
        return half + b * (1 - 2 * half)

    def gradient_step(w_t, gate_t, up_t):
        b, i = pl.program_id(0), pl.program_id(1)

        @pl.when(jnp.logical_and(b == 0, i == 0))
        def _():
            near_first()

        @pl.when(jnp.logical_and(b == 1, i == 0))
        def _():
            far_first()

        h = taken(b)
        block = og_v[blocks(h)].reshape(half_rows, width)
        grad = lax.dot_general(
            block, w_t[...], (((1,), (1,)), ((), ())), preferred_element_type=jnp.float32
        )
        g = gate_t[...].astype(jnp.float32)
        u = up_t[...].astype(jnp.float32)
        sig = jax.nn.sigmoid(g)
        out = (span(h, half_rows), span(i, tile))
        gate_grad[out] = (grad * u * sig * (1.0 + g * (1.0 - sig))).astype(jnp.bfloat16)
        up_grad[out] = (grad * (g * sig)).astype(jnp.bfloat16)

        @pl.when(b == 1)
        def _():
            far_events(i)

    deep = pl.Buffered(3)
    spec = pl.BlockSpec((half_rows, tile), lambda b, i: (taken(b), i), pipeline_mode=deep)
    pltpu.emit_pipeline(
        gradient_step,
        grid=(2, tiles),
        in_specs=[pl.BlockSpec((tile, width), lambda b, i: (i, 0), pipeline_mode=deep), spec, spec],
    )(weight, gate, up)
    c_wait(1 - half)

    @pl.loop(0, steps)
    def _(i):
        lines = span(i, chunk)
        down_v[lines, :] = (down_v[lines, :].astype(jnp.float32) + own_product(i, 1 - half)).astype(jnp.bfloat16)
        spread(i, steps, h_second, lambda e: h_event(h_first + e), late=True)

    def far_columns(p):
        @pl.loop(p * (nt - 1), (p + 1) * (nt - 1))
        def _(e):
            b_event(e, False)

    far_columns(0)

    @pl.loop(0, steps)
    def _(i):
        e = i - (steps - 2 * h_third)

        @pl.when(jnp.logical_and(e >= 0, e < h_third))
        def _():
            h_event(steps - h_third + e)

        for j in range(1, nx):
            h_fwd(i, j, 1 - c).wait_recv()
        lines = span(i, chunk)
        total = down_v[lines, 0:part].astype(jnp.float32) + far_product(hidf_v, colsf_v, i, 0)
        down_v[lines, 0:part] = (total * scale).astype(jnp.bfloat16)

    for h in range(2):
        c_mate(h, c).wait_send()
    for j in range(1, nx):
        for k in range(2):
            x_copy(j, k).wait_send()

    @pl.loop(0, steps)
    def _(i):
        for j in range(1, nx):
            h_far(i, j).wait_send()
            h_fwd(i, j, c).wait_send()
        h_mate(i).wait_send()

    def z_sent(p):
        @pl.loop(0, nt)
        def _(o):
            for live, goes, to, a_sems, b_sems in (
                (jnp.logical_and(has_up, o <= t), to_up, t + 1, a_up, b_up),
                (jnp.logical_and(has_dn, o >= t), to_dn, t - 1, a_dn, b_dn),
            ):
                @pl.when(live)
                def _():
                    if p == 0:
                        for n in range(A_PIECES):
                            a_fwd(o, n, to, a_sems).wait_send()

                    @pl.when(goes(o, p))
                    def _():
                        for j in range(1, nx):
                            b_fwd(o, j, p, to, b_sems).wait_send()

    for p in range(PARTS):
        if p:
            far_columns(p)
        z_sent(p)

    @pl.when(outer)
    def _():
        for j in range(1, nx):
            for k in range(2):
                e_copy(j, k).wait_send()


def on_device(out_grad, gate_pre, up_pre, down_weight):
    nt, dp = lax.axis_size("tensor"), lax.axis_size("dp")
    nx = dp // 2
    _, rows, width = out_grad.shape
    _, tokens, hidden_width = gate_pre.shape
    chunk = next(n for n in (512, 256, 128) if hidden_width % n == 0)
    tile = min(chunk, 256)
    steps = hidden_width // chunk
    dev_cols = width // dp
    scale = 1.0 / math.sqrt(tokens * dp)
    bf16 = jnp.bfloat16
    dma = pltpu.SemaphoreType.DMA
    any_spec = pl.BlockSpec(memory_space=pl.ANY)
    vmem_spec = pl.BlockSpec(memory_space=pltpu.VMEM)
    kept = pl.pallas_call(
        functools.partial(exchange, nt, nx, chunk, tile, scale),
        out_shape=(
            pltpu.VMEM((tokens, hidden_width), bf16),
            pltpu.VMEM((tokens, hidden_width), bf16),
            pltpu.VMEM((hidden_width, dev_cols), bf16),
            pltpu.VMEM((steps, 2 * nx - 2, tokens, chunk), bf16),
            pltpu.VMEM((2 * nx - 2, nt, rows, dev_cols), bf16),
        ),
        in_specs=[any_spec] * 4,
        out_specs=[vmem_spec] * 5,
        scratch_shapes=[
            pltpu.VMEM((nt, rows, width), bf16),
            pltpu.VMEM((steps, 2, tokens, chunk), bf16),
            pltpu.VMEM((2, nt, rows, dev_cols), bf16),
            dma,
            dma((nt, A_PIECES)),
            dma((nt, A_PIECES)),
            dma((nt, A_PIECES)),
            dma((nx, 2)),
            dma((2 * nx - 2,)),
            dma((nx, 2)),
            dma((2 * nx - 2,)),
            dma((nt, nx, PARTS)),
            dma((nt, nx, PARTS)),
            dma((nt, nx, PARTS)),
            dma((steps,)),
            dma((steps,)),
            dma((nx, steps)),
            dma((2 * nx, steps)),
            dma((nx, steps)),
            dma((2,)),
            dma((2,)),
            dma((2,)),
        ],
        compiler_params=pltpu.CompilerParams(
            collective_id=0, has_side_effects=True, vmem_limit_bytes=31 * 2**20
        ),
    )(out_grad[0], gate_pre[0], up_pre[0], down_weight)
    gate_grad, up_grad, down_grad = pl.pallas_call(
        functools.partial(finish, scale),
        out_shape=(
            jax.ShapeDtypeStruct((tokens, hidden_width), bf16),
            jax.ShapeDtypeStruct((tokens, hidden_width), bf16),
            jax.ShapeDtypeStruct((hidden_width, dev_cols), bf16),
        ),
        in_specs=[vmem_spec] * 5,
        out_specs=[any_spec] * 3,
        scratch_shapes=[pltpu.VMEM((hidden_width, dev_cols // PARTS), bf16), dma((3,)), dma((steps,))],
        compiler_params=pltpu.CompilerParams(vmem_limit_bytes=8 * 2**20),
    )(*kept)
    return (gate_grad[None], up_grad[None], down_grad)


def solution(mesh):
    return jax.shard_map(
        on_device,
        mesh=mesh,
        in_specs=(
            P("dp", ("groups", "tensor"), None),
            P("dp", "groups", "tensor"),
            P("dp", "groups", "tensor"),
            P("tensor", None),
        ),
        out_specs=(
            P("dp", "groups", "tensor"),
            P("dp", "groups", "tensor"),
            P(("groups", "tensor"), "dp"),
        ),
        check_vma=False,
    )
```

```python
import functools
import math

import jax
import jax.numpy as jnp
from jax import lax
from jax.experimental import pallas as pl
from jax.experimental.pallas import tpu as pltpu
from jax.sharding import PartitionSpec as P

A_PIECES = 2
PARTS = 2
MESH = pl.DeviceIdType.MESH


def far_product(hid_v, cols_v, i, p):
    groups, tokens, chunk = hid_v.shape[1:]
    part = cols_v.shape[3] // PARTS
    k = groups * tokens
    return lax.dot_general(
        hid_v[i].reshape(k, chunk), cols_v[:, :, :, p * part:(p + 1) * part].reshape(k, part),
        (((0,), (0,)), ((), ())), preferred_element_type=jnp.float32,
    )


def finish(scale, gate_v, up_v, down_v, hid_v, cols_v, gate_grad, up_grad, down_grad, last_v, sems, last_sems):
    steps, chunk = hid_v.shape[0], hid_v.shape[3]
    part = down_v.shape[1] // PARTS
    copies = [
        pltpu.make_async_copy(gate_v, gate_grad, sems.at[0]),
        pltpu.make_async_copy(up_v, up_grad, sems.at[1]),
        pltpu.make_async_copy(down_v.at[:, pl.ds(0, part)], down_grad.at[:, pl.ds(0, part)], sems.at[2]),
    ]
    for copy in copies:
        copy.start()

    def last_copy(i):
        lines = pl.ds(i * chunk, chunk)
        return pltpu.make_async_copy(last_v.at[lines], down_grad.at[lines, pl.ds(part, part)], last_sems.at[i])

    for i in range(steps):
        lines = slice(i * chunk, (i + 1) * chunk)
        total = down_v[lines, part:].astype(jnp.float32) + far_product(hid_v, cols_v, i, 1)
        last_v[lines, :] = (total * scale).astype(jnp.bfloat16)
        last_copy(i).start()
    for i in range(steps):
        last_copy(i).wait()
    for copy in copies:
        copy.wait()


def exchange(
    nt, nx, chunk, tile, scale,
    og, gate, up, weight,
    gate_grad, up_grad, down_v, hidf_v, colsf_v,
    og_v, hid_v, cols_v,
    own_sem, a_recv, a_up, a_dn, x_send, x_recv, e_send, e_recv, b_recv, b_up, b_dn,
    hm_send, hm_recv, hx_send, hf_recv, hf_send,
    c_local, c_send, c_recv,
):
    t = lax.axis_index("tensor")
    d = lax.axis_index("dp")
    x, c = d // 2, d % 2
    mate = x * 2 + (1 - c)
    rows, width = og.shape
    tokens, hidden_width = gate.shape
    dev_cols = width // (2 * nx)
    part = dev_cols // PARTS
    a_cols = width // A_PIECES
    steps = hidden_width // chunk
    tiles = hidden_width // tile
    half_blocks = nt // 2
    half_rows = half_blocks * rows
    near = max(1, half_blocks - 1)
    has_up, has_dn = t < nt - 1, t > 0
    inner = jnp.logical_and(has_up, has_dn)
    outer = jnp.logical_not(inner)

    def span(i, size):
        return pl.ds(pl.multiple_of(i * size, size), size)

    def remote(src, dst, send, recv, **where):
        return pltpu.make_async_remote_copy(
            src_ref=src, dst_ref=dst, send_sem=send, recv_sem=recv,
            device_id=where, device_id_type=MESH,
        )

    def other(j):
        return (x + j) % nx

    def far(j, core):
        return 2 * (j - 1) + core

    barrier = pltpu.get_barrier_semaphore()

    @pl.when(has_up)
    def _():
        pl.semaphore_signal(barrier, 1, device_id={"tensor": t + 1}, device_id_type=MESH)

    @pl.when(has_dn)
    def _():
        pl.semaphore_signal(barrier, 1, device_id={"tensor": t - 1}, device_id_type=MESH)

    pl.semaphore_signal(barrier, 1, device_id={"dp": mate}, device_id_type=MESH)
    for j in range(1, nx):
        for k in range(2):
            pl.semaphore_signal(barrier, 1, device_id={"dp": other(j) * 2 + k}, device_id_type=MESH)

    @pl.when(inner)
    def _():
        pl.semaphore_wait(barrier, 2 * nx + 1)

    @pl.when(outer)
    def _():
        pl.semaphore_wait(barrier, 2 * nx)

    def a_copy(src, o, p, to, sems):
        return remote(src, og_v.at[o, :, span(p, a_cols)], sems.at[o, p], a_recv.at[o, p], tensor=to)

    def a_fwd(o, p, to, sems):
        return a_copy(og_v.at[o, :, span(p, a_cols)], o, p, to, sems)

    def a_event(e):
        k, p = e // A_PIECES + 1, e % A_PIECES

        @pl.when(t - k >= 0)
        def _():
            a_fwd(t - k, p, t + 1, a_up).wait_recv()

            @pl.when(has_up)
            def _():
                a_fwd(t - k, p, t + 1, a_up).start()

        @pl.when(t + k < nt)
        def _():
            a_fwd(t + k, p, t - 1, a_dn).wait_recv()

            @pl.when(has_dn)
            def _():
                a_fwd(t + k, p, t - 1, a_dn).start()

    def x_copy(j, k):
        xo = other(j)
        slot = far(nx - j, c)
        return remote(
            og.at[:, span(xo * 2 + k, dev_cols)], colsf_v.at[slot, t],
            x_send.at[j, k], x_recv.at[slot], dp=xo * 2 + k,
        )

    def x_arrived(j, core):
        ref = colsf_v.at[far(j, core), t]
        return remote(ref, ref, x_send.at[j, core], x_recv.at[far(j, core)], dp=mate)

    beside = jnp.where(has_up, t + 1, t - 1)
    last = PARTS - 1

    def e_copy(j, k):
        xo = other(j)
        slot = far(nx - j, c)
        return remote(
            og_v.at[beside, :, span((xo * 2 + k) * PARTS + last, part)],
            colsf_v.at[slot, beside, :, span(last, part)],
            e_send.at[j, k], e_recv.at[slot], dp=xo * 2 + k,
        )

    def e_arrived(j, core):
        ref = colsf_v.at[far(j, core), beside, :, span(last, part)]
        return remote(ref, ref, e_send.at[j, core], e_recv.at[far(j, core)], dp=mate)

    def b_fwd(o, j, p, to, sems):
        ref = colsf_v.at[pl.ds(far(j, 0), 2), o, :, span(p, part)]
        return remote(ref, ref, sems.at[o, j, p], b_recv.at[o, j, p], tensor=to)

    def to_up(o, p):
        over_x = jnp.logical_and(jnp.logical_and(t + 1 == nt - 1, o == t), p == last)
        return jnp.logical_and(has_up, jnp.logical_not(over_x))

    def to_dn(o, p):
        over_x = jnp.logical_and(jnp.logical_and(t - 1 == 0, o == t), p == last)
        return jnp.logical_and(has_dn, jnp.logical_not(over_x))

    def b_own(p):
        for j in range(1, nx):
            @pl.when(to_up(t, p))
            def _():
                b_fwd(t, j, p, t + 1, b_up).start()

            @pl.when(to_dn(t, p))
            def _():
                b_fwd(t, j, p, t - 1, b_dn).start()

    def blocks(h):
        return pl.ds(h * half_blocks, half_blocks)

    def c_local_copy(h):
        return pltpu.make_async_copy(
            og_v.at[blocks(h), :, span(d, dev_cols)], cols_v.at[c, blocks(h)], c_local.at[h]
        )

    def c_mate(h, core):
        return remote(
            og_v.at[blocks(h), :, span(mate, dev_cols)], cols_v.at[core, blocks(h)],
            c_send.at[h], c_recv.at[h], dp=mate,
        )

    def c_share(h):
        c_local_copy(h).start()
        c_mate(h, c).start()

    def c_wait(h):
        c_local_copy(h).wait()
        c_mate(h, 1 - c).wait_recv()

    def b_event(e, onward):
        p, k = e // (nt - 1), e % (nt - 1) + 1
        if onward:
            @pl.when(jnp.logical_and(inner, jnp.logical_and(k == 1, p > 0)))
            def _():
                b_own(p)
        over_x = jnp.logical_and(k == 1, p == last)
        for o, live, to, sems in (
            (t - k, t - k >= 0, t + 1, b_up),
            (t + k, t + k < nt, t - 1, b_dn),
        ):
            @pl.when(jnp.logical_and(live, inner if onward else outer))
            def _():
                for j in range(1, nx):
                    if onward:
                        b_fwd(o, j, p, to, sems).wait_recv()
                        b_fwd(o, j, p, to, sems).start()
                    else:
                        @pl.when(over_x)
                        def _():
                            for core in range(2):
                                e_arrived(j, core).wait_recv()

                        @pl.when(jnp.logical_not(over_x))
                        def _():
                            b_fwd(o, j, p, to, sems).wait_recv()

    def h_far(i, j):
        return remote(
            hid_v.at[i, c], hidf_v.at[i, far(nx - j, c)], hx_send.at[j, i], hf_recv.at[far(nx - j, c), i],
            dp=other(j) * 2 + c,
        )

    def h_mate(i):
        return remote(hid_v.at[i, c], hid_v.at[i, c], hm_send.at[i], hm_recv.at[i], dp=mate)

    def h_fwd(i, j, core):
        ref = hidf_v.at[i, far(j, core)]
        return remote(ref, ref, hf_send.at[j, i], hf_recv.at[far(j, core), i], dp=mate)

    def h_event(i):
        for j in range(1, nx):
            h_fwd(i, j, c).wait_recv()
            h_fwd(i, j, c).start()

    own = pltpu.make_async_copy(og, og_v.at[t], own_sem)
    own.start()
    for j in range(1, nx):
        for k in range(2):
            x_copy(j, k).start()
    for p in range(A_PIECES):
        @pl.when(has_up)
        def _():
            a_copy(og.at[:, span(p, a_cols)], t, p, t + 1, a_up).start()

        @pl.when(has_dn)
        def _():
            a_copy(og.at[:, span(p, a_cols)], t, p, t - 1, a_dn).start()

    def hidden_step(gate_t, up_t):
        i = pl.program_id(0)
        g = gate_t[...].astype(jnp.float32)
        u = up_t[...].astype(jnp.float32)
        hid_v[i, c] = (g * jax.nn.sigmoid(g) * u).astype(jnp.bfloat16)
        for j in range(1, nx):
            h_far(i, j).start()
        h_mate(i).start()

    column_spec = pl.BlockSpec((tokens, chunk), lambda i: (0, i))
    pltpu.emit_pipeline(hidden_step, grid=(steps,), in_specs=[column_spec, column_spec])(gate, up)

    def spread(i, total, count, event, late=False):
        per_step = -(-count // total)
        for n in range(per_step):
            e = i * per_step + n - ((total * per_step - count) if late else 0)

            @pl.when(jnp.logical_and(e >= 0, e < count))
            def _():
                event(e)

    h_third = max(1, steps // 7)
    h_second = 2 * h_third
    h_first = steps - h_second - h_third
    b_count = PARTS * (nt - 1)
    half = t // half_blocks
    a_count = (nt - 1) * A_PIECES
    a_near = near * A_PIECES
    a_mid = min(a_count - a_near, A_PIECES)

    def near_first():
        @pl.loop(0, a_near)
        def _(e):
            a_event(e)

        own.wait()
        c_share(half)

        @pl.when(outer)
        def _():
            for j in range(1, nx):
                for k in range(2):
                    e_copy(j, k).start()
        for j in range(1, nx):
            for k in range(2):
                x_arrived(j, k).wait_recv()

        @pl.when(outer)
        def _():
            for p in range(PARTS):
                b_own(p)

    def own_product(i, h):
        k = 2 * half_rows
        return lax.dot_general(
            hid_v[i, :, span(h, half_rows)].reshape(k, chunk), cols_v[:, blocks(h)].reshape(k, dev_cols),
            (((0,), (0,)), ((), ())), preferred_element_type=jnp.float32,
        )

    def far_first():
        c_wait(half)

        @pl.loop(0, steps)
        def _(i):
            remote(hid_v.at[i, 1 - c], hid_v.at[i, 1 - c], hm_send.at[i], hm_recv.at[i], dp=mate).wait_recv()
            down_v[span(i, chunk), :] = own_product(i, half).astype(jnp.bfloat16)
            spread(i, steps, a_mid, lambda e: a_event(a_near + e), late=True)

        @pl.loop(a_near + a_mid, a_count)
        def _(e):
            a_event(e)

        c_share(1 - half)

        @pl.when(inner)
        def _():
            b_own(0)

    def far_events(i):
        def event(e):
            @pl.when(e < b_count)
            def _():
                b_event(e, True)

            @pl.when(e >= b_count)
            def _():
                h_event(e - b_count)

        spread(i, tiles, b_count + h_first, event)

    def taken(b):
        return half + b * (1 - 2 * half)

    def gradient_step(w_t, gate_t, up_t):
        b, i = pl.program_id(0), pl.program_id(1)

        @pl.when(jnp.logical_and(b == 0, i == 0))
        def _():
            near_first()

        @pl.when(jnp.logical_and(b == 1, i == 0))
        def _():
            far_first()

        h = taken(b)
        block = og_v[blocks(h)].reshape(half_rows, width)
        grad = lax.dot_general(
            block, w_t[...], (((1,), (1,)), ((), ())), preferred_element_type=jnp.float32
        )
        g = gate_t[...].astype(jnp.float32)
        u = up_t[...].astype(jnp.float32)
        sig = jax.nn.sigmoid(g)
        out = (span(h, half_rows), span(i, tile))
        gate_grad[out] = (grad * u * sig * (1.0 + g * (1.0 - sig))).astype(jnp.bfloat16)
        up_grad[out] = (grad * (g * sig)).astype(jnp.bfloat16)

        @pl.when(b == 1)
        def _():
            far_events(i)

    deep = pl.Buffered(3)
    spec = pl.BlockSpec((half_rows, tile), lambda b, i: (taken(b), i), pipeline_mode=deep)
    pltpu.emit_pipeline(
        gradient_step,
        grid=(2, tiles),
        in_specs=[pl.BlockSpec((tile, width), lambda b, i: (i, 0), pipeline_mode=deep), spec, spec],
    )(weight, gate, up)
    c_wait(1 - half)

    @pl.loop(0, steps)
    def _(i):
        lines = span(i, chunk)
        down_v[lines, :] = (down_v[lines, :].astype(jnp.float32) + own_product(i, 1 - half)).astype(jnp.bfloat16)
        spread(i, steps, h_second, lambda e: h_event(h_first + e), late=True)

    def far_columns(p):
        @pl.loop(p * (nt - 1), (p + 1) * (nt - 1))
        def _(e):
            b_event(e, False)

    far_columns(0)

    @pl.loop(0, steps)
    def _(i):
        e = i - (steps - 2 * h_third)

        @pl.when(jnp.logical_and(e >= 0, e < h_third))
        def _():
            h_event(steps - h_third + e)

        for j in range(1, nx):
            h_fwd(i, j, 1 - c).wait_recv()
        lines = span(i, chunk)
        total = down_v[lines, 0:part].astype(jnp.float32) + far_product(hidf_v, colsf_v, i, 0)
        down_v[lines, 0:part] = (total * scale).astype(jnp.bfloat16)

    for h in range(2):
        c_mate(h, c).wait_send()
    for j in range(1, nx):
        for k in range(2):
            x_copy(j, k).wait_send()

    @pl.loop(0, steps)
    def _(i):
        for j in range(1, nx):
            h_far(i, j).wait_send()
            h_fwd(i, j, c).wait_send()
        h_mate(i).wait_send()

    def z_sent(p):
        @pl.loop(0, nt)
        def _(o):
            for live, goes, to, a_sems, b_sems in (
                (jnp.logical_and(has_up, o <= t), to_up, t + 1, a_up, b_up),
                (jnp.logical_and(has_dn, o >= t), to_dn, t - 1, a_dn, b_dn),
            ):
                @pl.when(live)
                def _():
                    if p == 0:
                        for n in range(A_PIECES):
                            a_fwd(o, n, to, a_sems).wait_send()

                    @pl.when(goes(o, p))
                    def _():
                        for j in range(1, nx):
                            b_fwd(o, j, p, to, b_sems).wait_send()

    for p in range(PARTS):
        if p:
            far_columns(p)
        z_sent(p)

    @pl.when(outer)
    def _():
        for j in range(1, nx):
            for k in range(2):
                e_copy(j, k).wait_send()


def on_device(out_grad, gate_pre, up_pre, down_weight):
    nt, dp = lax.axis_size("tensor"), lax.axis_size("dp")
    nx = dp // 2
    _, rows, width = out_grad.shape
    _, tokens, hidden_width = gate_pre.shape
    chunk = next(n for n in (512, 256, 128) if hidden_width % n == 0)
    tile = min(chunk, 256)
    steps = hidden_width // chunk
    dev_cols = width // dp
    scale = 1.0 / math.sqrt(tokens * dp)
    bf16 = jnp.bfloat16
    dma = pltpu.SemaphoreType.DMA
    any_spec = pl.BlockSpec(memory_space=pl.ANY)
    vmem_spec = pl.BlockSpec(memory_space=pltpu.VMEM)
    kept = pl.pallas_call(
        functools.partial(exchange, nt, nx, chunk, tile, scale),
        out_shape=(
            pltpu.VMEM((tokens, hidden_width), bf16),
            pltpu.VMEM((tokens, hidden_width), bf16),
            pltpu.VMEM((hidden_width, dev_cols), bf16),
            pltpu.VMEM((steps, 2 * nx - 2, tokens, chunk), bf16),
            pltpu.VMEM((2 * nx - 2, nt, rows, dev_cols), bf16),
        ),
        in_specs=[any_spec] * 4,
        out_specs=[vmem_spec] * 5,
        scratch_shapes=[
            pltpu.VMEM((nt, rows, width), bf16),
            pltpu.VMEM((steps, 2, tokens, chunk), bf16),
            pltpu.VMEM((2, nt, rows, dev_cols), bf16),
            dma,
            dma((nt, A_PIECES)),
            dma((nt, A_PIECES)),
            dma((nt, A_PIECES)),
            dma((nx, 2)),
            dma((2 * nx - 2,)),
            dma((nx, 2)),
            dma((2 * nx - 2,)),
            dma((nt, nx, PARTS)),
            dma((nt, nx, PARTS)),
            dma((nt, nx, PARTS)),
            dma((steps,)),
            dma((steps,)),
            dma((nx, steps)),
            dma((2 * nx, steps)),
            dma((nx, steps)),
            dma((2,)),
            dma((2,)),
            dma((2,)),
        ],
        compiler_params=pltpu.CompilerParams(
            collective_id=0, has_side_effects=True, vmem_limit_bytes=31 * 2**20
        ),
    )(out_grad[0], gate_pre[0], up_pre[0], down_weight)
    gate_grad, up_grad, down_grad = pl.pallas_call(
        functools.partial(finish, scale),
        out_shape=(
            jax.ShapeDtypeStruct((tokens, hidden_width), bf16),
            jax.ShapeDtypeStruct((tokens, hidden_width), bf16),
            jax.ShapeDtypeStruct((hidden_width, dev_cols), bf16),
        ),
        in_specs=[vmem_spec] * 5,
        out_specs=[any_spec] * 3,
        scratch_shapes=[pltpu.VMEM((hidden_width, dev_cols // PARTS), bf16), dma((3,)), dma((steps,))],
        compiler_params=pltpu.CompilerParams(vmem_limit_bytes=8 * 2**20),
    )(*kept)
    return (gate_grad[None], up_grad[None], down_grad)


def solution(mesh):
    return jax.shard_map(
        on_device,
        mesh=mesh,
        in_specs=(
            P("dp", ("groups", "tensor"), None),
            P("dp", "groups", "tensor"),
            P("dp", "groups", "tensor"),
            P("tensor", None),
        ),
        out_specs=(
            P("dp", "groups", "tensor"),
            P("dp", "groups", "tensor"),
            P(("groups", "tensor"), "dp"),
        ),
        check_vma=False,
    )
```

```python
import functools
import math

import jax
import jax.numpy as jnp
from jax import lax
from jax.experimental import pallas as pl
from jax.experimental.pallas import tpu as pltpu
from jax.sharding import PartitionSpec as P

A_PIECES = 2
PARTS = 2
MESH = pl.DeviceIdType.MESH


def far_product(hid_v, cols_v, i, p):
    groups, tokens, chunk = hid_v.shape[1:]
    part = cols_v.shape[3] // PARTS
    k = groups * tokens
    return lax.dot_general(
        hid_v[i].reshape(k, chunk), cols_v[:, :, :, p * part:(p + 1) * part].reshape(k, part),
        (((0,), (0,)), ((), ())), preferred_element_type=jnp.float32,
    )


def finish(scale, gate_v, up_v, down_v, hid_v, cols_v, gate_grad, up_grad, down_grad, last_v, sems, last_sems):
    steps, chunk = hid_v.shape[0], hid_v.shape[3]
    part = down_v.shape[1] // PARTS
    copies = [
        pltpu.make_async_copy(gate_v, gate_grad, sems.at[0]),
        pltpu.make_async_copy(up_v, up_grad, sems.at[1]),
        pltpu.make_async_copy(down_v.at[:, pl.ds(0, part)], down_grad.at[:, pl.ds(0, part)], sems.at[2]),
    ]
    for copy in copies:
        copy.start()

    def last_copy(i):
        lines = pl.ds(i * chunk, chunk)
        return pltpu.make_async_copy(last_v.at[lines], down_grad.at[lines, pl.ds(part, part)], last_sems.at[i])

    for i in range(steps):
        lines = slice(i * chunk, (i + 1) * chunk)
        total = down_v[lines, part:].astype(jnp.float32) + far_product(hid_v, cols_v, i, 1)
        last_v[lines, :] = (total * scale).astype(jnp.bfloat16)
        last_copy(i).start()
    for i in range(steps):
        last_copy(i).wait()
    for copy in copies:
        copy.wait()


def exchange(
    nt, nx, chunk, tile, scale,
    og, gate, up, weight,
    gate_grad, up_grad, down_v, hidf_v, colsf_v,
    og_v, hid_v, cols_v,
    own_sem, a_recv, a_up, a_dn, x_send, x_recv, e_send, e_recv, b_recv, b_up, b_dn,
    hm_send, hm_recv, hx_send, hf_recv, hf_send,
    c_local, c_send, c_recv,
):
    t = lax.axis_index("tensor")
    d = lax.axis_index("dp")
    x, c = d // 2, d % 2
    mate = x * 2 + (1 - c)
    rows, width = og.shape
    tokens, hidden_width = gate.shape
    dev_cols = width // (2 * nx)
    part = dev_cols // PARTS
    a_cols = width // A_PIECES
    steps = hidden_width // chunk
    tiles = hidden_width // tile
    half_blocks = nt // 2
    half_rows = half_blocks * rows
    near = max(1, half_blocks - 1)
    has_up, has_dn = t < nt - 1, t > 0
    inner = jnp.logical_and(has_up, has_dn)
    outer = jnp.logical_not(inner)

    def span(i, size):
        return pl.ds(pl.multiple_of(i * size, size), size)

    def remote(src, dst, send, recv, **where):
        return pltpu.make_async_remote_copy(
            src_ref=src, dst_ref=dst, send_sem=send, recv_sem=recv,
            device_id=where, device_id_type=MESH,
        )

    def other(j):
        return (x + j) % nx

    def far(j, core):
        return 2 * (j - 1) + core

    barrier = pltpu.get_barrier_semaphore()

    @pl.when(has_up)
    def _():
        pl.semaphore_signal(barrier, 1, device_id={"tensor": t + 1}, device_id_type=MESH)

    @pl.when(has_dn)
    def _():
        pl.semaphore_signal(barrier, 1, device_id={"tensor": t - 1}, device_id_type=MESH)

    pl.semaphore_signal(barrier, 1, device_id={"dp": mate}, device_id_type=MESH)
    for j in range(1, nx):
        for k in range(2):
            pl.semaphore_signal(barrier, 1, device_id={"dp": other(j) * 2 + k}, device_id_type=MESH)

    @pl.when(inner)
    def _():
        pl.semaphore_wait(barrier, 2 * nx + 1)

    @pl.when(outer)
    def _():
        pl.semaphore_wait(barrier, 2 * nx)

    def a_copy(src, o, p, to, sems):
        return remote(src, og_v.at[o, :, span(p, a_cols)], sems.at[o, p], a_recv.at[o, p], tensor=to)

    def a_fwd(o, p, to, sems):
        return a_copy(og_v.at[o, :, span(p, a_cols)], o, p, to, sems)

    def a_event(e):
        k, p = e // A_PIECES + 1, e % A_PIECES

        @pl.when(t - k >= 0)
        def _():
            a_fwd(t - k, p, t + 1, a_up).wait_recv()

            @pl.when(has_up)
            def _():
                a_fwd(t - k, p, t + 1, a_up).start()

        @pl.when(t + k < nt)
        def _():
            a_fwd(t + k, p, t - 1, a_dn).wait_recv()

            @pl.when(has_dn)
            def _():
                a_fwd(t + k, p, t - 1, a_dn).start()

    def x_copy(j, k):
        xo = other(j)
        slot = far(nx - j, c)
        return remote(
            og.at[:, span(xo * 2 + k, dev_cols)], colsf_v.at[slot, t],
            x_send.at[j, k], x_recv.at[slot], dp=xo * 2 + k,
        )

    def x_arrived(j, core):
        ref = colsf_v.at[far(j, core), t]
        return remote(ref, ref, x_send.at[j, core], x_recv.at[far(j, core)], dp=mate)

    beside = jnp.where(has_up, t + 1, t - 1)
    last = PARTS - 1

    def e_copy(j, k):
        xo = other(j)
        slot = far(nx - j, c)
        return remote(
            og_v.at[beside, :, span((xo * 2 + k) * PARTS + last, part)],
            colsf_v.at[slot, beside, :, span(last, part)],
            e_send.at[j, k], e_recv.at[slot], dp=xo * 2 + k,
        )

    def e_arrived(j, core):
        ref = colsf_v.at[far(j, core), beside, :, span(last, part)]
        return remote(ref, ref, e_send.at[j, core], e_recv.at[far(j, core)], dp=mate)

    def b_fwd(o, j, p, to, sems):
        ref = colsf_v.at[pl.ds(far(j, 0), 2), o, :, span(p, part)]
        return remote(ref, ref, sems.at[o, j, p], b_recv.at[o, j, p], tensor=to)

    def to_up(o, p):
        over_x = jnp.logical_and(jnp.logical_and(t + 1 == nt - 1, o == t), p == last)
        return jnp.logical_and(has_up, jnp.logical_not(over_x))

    def to_dn(o, p):
        over_x = jnp.logical_and(jnp.logical_and(t - 1 == 0, o == t), p == last)
        return jnp.logical_and(has_dn, jnp.logical_not(over_x))

    def b_own(p):
        for j in range(1, nx):
            @pl.when(to_up(t, p))
            def _():
                b_fwd(t, j, p, t + 1, b_up).start()

            @pl.when(to_dn(t, p))
            def _():
                b_fwd(t, j, p, t - 1, b_dn).start()

    def blocks(h):
        return pl.ds(h * half_blocks, half_blocks)

    def c_local_copy(h):
        return pltpu.make_async_copy(
            og_v.at[blocks(h), :, span(d, dev_cols)], cols_v.at[c, blocks(h)], c_local.at[h]
        )

    def c_mate(h, core):
        return remote(
            og_v.at[blocks(h), :, span(mate, dev_cols)], cols_v.at[core, blocks(h)],
            c_send.at[h], c_recv.at[h], dp=mate,
        )

    def c_share(h):
        c_local_copy(h).start()
        c_mate(h, c).start()

    def c_wait(h):
        c_local_copy(h).wait()
        c_mate(h, 1 - c).wait_recv()

    def b_event(e, onward):
        p, k = e // (nt - 1), e % (nt - 1) + 1
        over_x = jnp.logical_and(k == 1, p == last)
        for o, live, to, sems in (
            (t - k, t - k >= 0, t + 1, b_up),
            (t + k, t + k < nt, t - 1, b_dn),
        ):
            @pl.when(jnp.logical_and(live, inner if onward else outer))
            def _():
                for j in range(1, nx):
                    if onward:
                        b_fwd(o, j, p, to, sems).wait_recv()
                        b_fwd(o, j, p, to, sems).start()
                    else:
                        @pl.when(over_x)
                        def _():
                            for core in range(2):
                                e_arrived(j, core).wait_recv()

                        @pl.when(jnp.logical_not(over_x))
                        def _():
                            b_fwd(o, j, p, to, sems).wait_recv()

    def h_far(i, j):
        return remote(
            hid_v.at[i, c], hidf_v.at[i, far(nx - j, c)], hx_send.at[j, i], hf_recv.at[far(nx - j, c), i],
            dp=other(j) * 2 + c,
        )

    def h_mate(i):
        return remote(hid_v.at[i, c], hid_v.at[i, c], hm_send.at[i], hm_recv.at[i], dp=mate)

    def h_fwd(i, j, core):
        ref = hidf_v.at[i, far(j, core)]
        return remote(ref, ref, hf_send.at[j, i], hf_recv.at[far(j, core), i], dp=mate)

    def h_event(i):
        for j in range(1, nx):
            h_fwd(i, j, c).wait_recv()
            h_fwd(i, j, c).start()

    own = pltpu.make_async_copy(og, og_v.at[t], own_sem)
    own.start()
    for j in range(1, nx):
        for k in range(2):
            x_copy(j, k).start()
    for p in range(A_PIECES):
        @pl.when(has_up)
        def _():
            a_copy(og.at[:, span(p, a_cols)], t, p, t + 1, a_up).start()

        @pl.when(has_dn)
        def _():
            a_copy(og.at[:, span(p, a_cols)], t, p, t - 1, a_dn).start()

    def hidden_step(gate_t, up_t):
        i = pl.program_id(0)
        g = gate_t[...].astype(jnp.float32)
        u = up_t[...].astype(jnp.float32)
        hid_v[i, c] = (g * jax.nn.sigmoid(g) * u).astype(jnp.bfloat16)
        for j in range(1, nx):
            h_far(i, j).start()
        h_mate(i).start()

    column_spec = pl.BlockSpec((tokens, chunk), lambda i: (0, i))
    pltpu.emit_pipeline(hidden_step, grid=(steps,), in_specs=[column_spec, column_spec])(gate, up)

    def spread(i, total, count, event, late=False):
        per_step = -(-count // total)
        for n in range(per_step):
            e = i * per_step + n - ((total * per_step - count) if late else 0)

            @pl.when(jnp.logical_and(e >= 0, e < count))
            def _():
                event(e)

    h_third = max(1, steps // 7)
    h_second = 2 * h_third
    h_first = steps - h_second - h_third
    b_count = PARTS * (nt - 1)
    half = t // half_blocks
    a_count = (nt - 1) * A_PIECES
    a_near = near * A_PIECES
    a_mid = min(a_count - a_near, A_PIECES)

    def near_first():
        @pl.loop(0, a_near)
        def _(e):
            a_event(e)

        own.wait()
        c_share(half)

        @pl.when(outer)
        def _():
            for j in range(1, nx):
                for k in range(2):
                    e_copy(j, k).start()
        for j in range(1, nx):
            for k in range(2):
                x_arrived(j, k).wait_recv()

        @pl.when(outer)
        def _():
            for p in range(PARTS):
                b_own(p)

    def own_product(i, h):
        k = 2 * half_rows
        return lax.dot_general(
            hid_v[i, :, span(h, half_rows)].reshape(k, chunk), cols_v[:, blocks(h)].reshape(k, dev_cols),
            (((0,), (0,)), ((), ())), preferred_element_type=jnp.float32,
        )

    def far_first():
        c_wait(half)

        @pl.loop(0, steps)
        def _(i):
            remote(hid_v.at[i, 1 - c], hid_v.at[i, 1 - c], hm_send.at[i], hm_recv.at[i], dp=mate).wait_recv()
            down_v[span(i, chunk), :] = own_product(i, half).astype(jnp.bfloat16)
            spread(i, steps, a_mid, lambda e: a_event(a_near + e), late=True)

        @pl.loop(a_near + a_mid, a_count)
        def _(e):
            a_event(e)

        c_share(1 - half)

        @pl.when(inner)
        def _():
            for p in range(PARTS):
                b_own(p)

    def far_events(i):
        def event(e):
            @pl.when(e < b_count)
            def _():
                b_event(e, True)

            @pl.when(e >= b_count)
            def _():
                h_event(e - b_count)

        spread(i, tiles, b_count + h_first, event)

    def taken(b):
        return half + b * (1 - 2 * half)

    def gradient_step(w_t, gate_t, up_t):
        b, i = pl.program_id(0), pl.program_id(1)

        @pl.when(jnp.logical_and(b == 0, i == 0))
        def _():
            near_first()

        @pl.when(jnp.logical_and(b == 1, i == 0))
        def _():
            far_first()

        h = taken(b)
        block = og_v[blocks(h)].reshape(half_rows, width)
        grad = lax.dot_general(
            block, w_t[...], (((1,), (1,)), ((), ())), preferred_element_type=jnp.float32
        )
        g = gate_t[...].astype(jnp.float32)
        u = up_t[...].astype(jnp.float32)
        sig = jax.nn.sigmoid(g)
        out = (span(h, half_rows), span(i, tile))
        gate_grad[out] = (grad * u * sig * (1.0 + g * (1.0 - sig))).astype(jnp.bfloat16)
        up_grad[out] = (grad * (g * sig)).astype(jnp.bfloat16)

        @pl.when(b == 1)
        def _():
            far_events(i)

    deep = pl.Buffered(3)
    spec = pl.BlockSpec((half_rows, tile), lambda b, i: (taken(b), i), pipeline_mode=deep)
    pltpu.emit_pipeline(
        gradient_step,
        grid=(2, tiles),
        in_specs=[pl.BlockSpec((tile, width), lambda b, i: (i, 0), pipeline_mode=deep), spec, spec],
    )(weight, gate, up)
    c_wait(1 - half)

    @pl.loop(0, steps)
    def _(i):
        lines = span(i, chunk)
        down_v[lines, :] = (down_v[lines, :].astype(jnp.float32) + own_product(i, 1 - half)).astype(jnp.bfloat16)
        spread(i, steps, h_second, lambda e: h_event(h_first + e), late=True)

    def far_columns(p):
        @pl.loop(p * (nt - 1), (p + 1) * (nt - 1))
        def _(e):
            b_event(e, False)

    far_columns(0)

    @pl.loop(0, steps)
    def _(i):
        e = i - (steps - 2 * h_third)

        @pl.when(jnp.logical_and(e >= 0, e < h_third))
        def _():
            h_event(steps - h_third + e)

        for j in range(1, nx):
            h_fwd(i, j, 1 - c).wait_recv()
        lines = span(i, chunk)
        total = down_v[lines, 0:part].astype(jnp.float32) + far_product(hidf_v, colsf_v, i, 0)
        down_v[lines, 0:part] = (total * scale).astype(jnp.bfloat16)

    for h in range(2):
        c_mate(h, c).wait_send()
    for j in range(1, nx):
        for k in range(2):
            x_copy(j, k).wait_send()

    @pl.loop(0, steps)
    def _(i):
        for j in range(1, nx):
            h_far(i, j).wait_send()
            h_fwd(i, j, c).wait_send()
        h_mate(i).wait_send()

    def z_sent(p):
        @pl.loop(0, nt)
        def _(o):
            for live, goes, to, a_sems, b_sems in (
                (jnp.logical_and(has_up, o <= t), to_up, t + 1, a_up, b_up),
                (jnp.logical_and(has_dn, o >= t), to_dn, t - 1, a_dn, b_dn),
            ):
                @pl.when(live)
                def _():
                    if p == 0:
                        for n in range(A_PIECES):
                            a_fwd(o, n, to, a_sems).wait_send()

                    @pl.when(goes(o, p))
                    def _():
                        for j in range(1, nx):
                            b_fwd(o, j, p, to, b_sems).wait_send()

    for p in range(PARTS):
        if p:
            far_columns(p)
        z_sent(p)

    @pl.when(outer)
    def _():
        for j in range(1, nx):
            for k in range(2):
                e_copy(j, k).wait_send()


def on_device(out_grad, gate_pre, up_pre, down_weight):
    nt, dp = lax.axis_size("tensor"), lax.axis_size("dp")
    nx = dp // 2
    _, rows, width = out_grad.shape
    _, tokens, hidden_width = gate_pre.shape
    chunk = next(n for n in (512, 256, 128) if hidden_width % n == 0)
    tile = min(chunk, 256)
    steps = hidden_width // chunk
    dev_cols = width // dp
    scale = 1.0 / math.sqrt(tokens * dp)
    bf16 = jnp.bfloat16
    dma = pltpu.SemaphoreType.DMA
    any_spec = pl.BlockSpec(memory_space=pl.ANY)
    vmem_spec = pl.BlockSpec(memory_space=pltpu.VMEM)
    kept = pl.pallas_call(
        functools.partial(exchange, nt, nx, chunk, tile, scale),
        out_shape=(
            pltpu.VMEM((tokens, hidden_width), bf16),
            pltpu.VMEM((tokens, hidden_width), bf16),
            pltpu.VMEM((hidden_width, dev_cols), bf16),
            pltpu.VMEM((steps, 2 * nx - 2, tokens, chunk), bf16),
            pltpu.VMEM((2 * nx - 2, nt, rows, dev_cols), bf16),
        ),
        in_specs=[any_spec] * 4,
        out_specs=[vmem_spec] * 5,
        scratch_shapes=[
            pltpu.VMEM((nt, rows, width), bf16),
            pltpu.VMEM((steps, 2, tokens, chunk), bf16),
            pltpu.VMEM((2, nt, rows, dev_cols), bf16),
            dma,
            dma((nt, A_PIECES)),
            dma((nt, A_PIECES)),
            dma((nt, A_PIECES)),
            dma((nx, 2)),
            dma((2 * nx - 2,)),
            dma((nx, 2)),
            dma((2 * nx - 2,)),
            dma((nt, nx, PARTS)),
            dma((nt, nx, PARTS)),
            dma((nt, nx, PARTS)),
            dma((steps,)),
            dma((steps,)),
            dma((nx, steps)),
            dma((2 * nx, steps)),
            dma((nx, steps)),
            dma((2,)),
            dma((2,)),
            dma((2,)),
        ],
        compiler_params=pltpu.CompilerParams(
            collective_id=0, has_side_effects=True, vmem_limit_bytes=31 * 2**20
        ),
    )(out_grad[0], gate_pre[0], up_pre[0], down_weight)
    gate_grad, up_grad, down_grad = pl.pallas_call(
        functools.partial(finish, scale),
        out_shape=(
            jax.ShapeDtypeStruct((tokens, hidden_width), bf16),
            jax.ShapeDtypeStruct((tokens, hidden_width), bf16),
            jax.ShapeDtypeStruct((hidden_width, dev_cols), bf16),
        ),
        in_specs=[vmem_spec] * 5,
        out_specs=[any_spec] * 3,
        scratch_shapes=[pltpu.VMEM((hidden_width, dev_cols // PARTS), bf16), dma((3,)), dma((steps,))],
        compiler_params=pltpu.CompilerParams(vmem_limit_bytes=8 * 2**20),
    )(*kept)
    return (gate_grad[None], up_grad[None], down_grad)


def solution(mesh):
    return jax.shard_map(
        on_device,
        mesh=mesh,
        in_specs=(
            P("dp", ("groups", "tensor"), None),
            P("dp", "groups", "tensor"),
            P("dp", "groups", "tensor"),
            P("tensor", None),
        ),
        out_specs=(
            P("dp", "groups", "tensor"),
            P("dp", "groups", "tensor"),
            P(("groups", "tensor"), "dp"),
        ),
        check_vma=False,
    )
```
